128 devices in a mesh: row: 16 (over z_lo, x, core), col: 8 (over y, z_hi).
Axes of the slice: x: 4, y: 4, z: 4 (z_hi: 2, z_lo: 2; z = z_hi * 2 + z_lo), core: 2. Of those that a mesh axis runs over, the one named last changes fastest.
Arguments:
- amplitudes: bfloat16 [7168, 7168], P('row', 'col'), as said below
- integrals: bfloat16 [7168, 7168], P('row', 'col'), as said below
- occ_energy: float32 [80], replicated, may hold values from -2 to -0.5
- vir_energy: float32 [1000], replicated, may hold values from 0.5 to 4
- pair_occ: int32 [7168], replicated, may hold values from 0 to 79, as said below
- pair_vir: int32 [7168], replicated, may hold values from 0 to 999, as said below
Outputs:
- updated: float32 [7168, 7168], P('row', 'col')
The draws below stay inside these ranges and needn't reach their ends.
Inputs may be any that keep to these rules, and one draw needn't show every extreme that they name: amplitudes is exactly symmetric. integrals is exactly symmetric. pair_occ[p] mod 8 equals pair_vir[p] mod 8 (one irrep block), and no pair (pair_occ[p], pair_vir[p]) occurs twice. `pair_vir`: see pair_occ.
All inputs are finite; a program needn't handle non-finite values.
Results may differ from the reference program's by a relative error of at most 0.0003.
Values may be sent and summed in bfloat16 or wider, within the bound.
No kernel may reach another device: no remote copies, remote signals or barrier semaphores. Data moves between devices by JAX's collectives and lax.ppermute only.
A program may use at most 128 MiB of HBM per device.

```python
import math
import jax
import jax.numpy as jnp

M = 7168
NOCC = 80
NVIR = 1000
NIRREP = 8


def symmetric_field(key):
    entries = jax.random.normal(key, (M, M), jnp.float32)
    return (entries + entries.T) * 0.7071


def draw_amplitudes(key, part):
    return symmetric_field(jax.random.fold_in(key, 11)).astype(jnp.bfloat16)


def draw_integrals(key, part):
    return (symmetric_field(jax.random.fold_in(key, 12)) * (1.0 / math.sqrt(M))).astype(jnp.bfloat16)


def pair_index(key):
    pair_count = NOCC * (NVIR // NIRREP)
    shuffled = jax.random.permutation(jax.random.fold_in(key, 7), jnp.arange(1, pair_count - 1, dtype=jnp.int32))[:M - 2]
    chosen = jnp.concatenate([jnp.array([0, pair_count - 1], dtype=jnp.int32), shuffled])
    return jax.random.permutation(jax.random.fold_in(key, 8), chosen)


def draw_pair_occ(key, part):
    return (pair_index(key) // (NVIR // NIRREP)).astype(jnp.int32)


def draw_pair_vir(key, part):
    indices = pair_index(key)
    occupied = indices // (NVIR // NIRREP)
    return (NIRREP * (indices % (NVIR // NIRREP)) + occupied % NIRREP).astype(jnp.int32)


def setup_inputs(seed: int = 0) -> dict:
    arg_keys = jax.random.split(jax.random.key(seed), 7)
    return {
        "amplitudes": draw_amplitudes(jax.random.fold_in(arg_keys[6], 71), 0),
        "integrals": draw_integrals(jax.random.fold_in(arg_keys[6], 71), 0),
        "occ_energy": jnp.clip(jax.random.uniform(arg_keys[2], (NOCC,), jnp.float32, -2.0, -0.5), -2.0, -0.5),
        "vir_energy": jnp.clip(jax.random.uniform(arg_keys[3], (NVIR,), jnp.float32, 0.5, 4.0), 0.5, 4.0),
        "pair_occ": draw_pair_occ(jax.random.fold_in(arg_keys[6], 71), 0),
        "pair_vir": draw_pair_vir(jax.random.fold_in(arg_keys[6], 71), 0),
    }


def reference(amplitudes, integrals, occ_energy, vir_energy, pair_occ, pair_vir):
    product = jnp.dot(amplitudes, integrals, preferred_element_type=jnp.float32)
    pair_gap = occ_energy[pair_occ] - vir_energy[pair_vir]
    return (product + product.T) / (pair_gap[:, None] + pair_gap[None, :])
```

```python
import jax
import jax.numpy as jnp
from jax import lax
from jax.experimental import pallas as pl
from jax.experimental.pallas import tpu as pltpu
from jax.sharding import PartitionSpec as P

Z_LO, X, CORE, Y, Z_HI = 2, 4, 2, 4, 2
AXES = ("row", "col")
LEVELS = 15


def device_index(z_lo, x, core, y, z_hi):
    return ((z_lo * X + x) * CORE + core) * (Y * Z_HI) + y * Z_HI + z_hi


def places():
    for z_lo in range(Z_LO):
        for x in range(X):
            for core in range(CORE):
                for y in range(Y):
                    for z_hi in range(Z_HI):
                        yield z_lo, x, core, y, z_hi


def send(block, target):
    pairs = [(device_index(*place), device_index(*target(*place))) for place in places()]
    return lax.ppermute(block, AXES, pairs)


def along_x(step):
    return lambda z_lo, x, core, y, z_hi: (z_lo, (x + step) % X, core, y, z_hi)


def along_y(step):
    return lambda z_lo, x, core, y, z_hi: (z_lo, x, core, (y + step) % Y, z_hi)


def across_z_lo(z_lo, x, core, y, z_hi):
    return 1 - z_lo, x, core, y, z_hi


def across_z_hi(z_lo, x, core, y, z_hi):
    return z_lo, x, core, y, 1 - z_hi


def across_core(z_lo, x, core, y, z_hi):
    return z_lo, x, 1 - core, y, z_hi


def mirrored(flip):
    def target(z_lo, x, core, y, z_hi):
        chip_row, chip_col = z_lo * X + x, y * Z_HI + z_hi
        return chip_col // X, chip_col % X, core ^ flip, chip_row // Z_HI, chip_row % Z_HI

    return target


def ring(block, along):
    half = block.shape[0] // 2
    before = send(block, along(1))
    after = send(block, along(-1))
    top = send(before[:half], along(1))
    bottom = send(after[half:], along(-1))
    return [(block,), (after,), (top, bottom), (before,)]


def gather(block, along, across):
    return ring(block, along) + ring(send(block, across), along)


def lookup(energies, orbital_index):
    labels = jnp.arange(energies.shape[0], dtype=jnp.int32)
    picked = jnp.where(orbital_index[:, None] == labels[None, :], energies[None, :], 0.0)
    return jnp.sum(picked, axis=1)


def product_kernel(counts_a, counts_b, *refs):
    total_a, total_b = sum(counts_a), sum(counts_b)
    a_parts, b_parts, rest = refs[:total_a], refs[total_a:total_a + total_b], refs[total_a + total_b:]
    out_ref, left, right, acc, sem_a, sem_b = rest
    row, col = lax.axis_index("row"), lax.axis_index("col")
    z_lo, x, core = row // (X * CORE), (row // CORE) % X, row % CORE
    y, z_hi = col // Z_HI, col % Z_HI
    rows, depth = left.shape[1], left.shape[2]
    copies_a, copies_b = [], []
    at = 0
    for slot, count in enumerate(counts_a):
        part = rows // count
        for i in range(count):
            copies_a.append(pltpu.make_async_copy(
                a_parts[at], left.at[slot, pl.ds(i * part, part), :], sem_a.at[at]))
            at += 1
    half = depth // CORE
    at = 0
    for slot in range(len(counts_b) // 2):
        mine = []
        for other in range(CORE):
            base = pl.multiple_of((core if other == 0 else 1 - core) * half, half)
            count = counts_b[2 * slot + other]
            part = half // count
            for i in range(count):
                mine.append(pltpu.make_async_copy(
                    b_parts[at], right.at[slot, pl.ds(base + i * part, part), :], sem_b.at[at]))
                at += 1
        copies_b.append(mine)
    for copy in copies_a:
        copy.start()
    for mine in copies_b:
        for copy in mine:
            copy.start()
    for copy in copies_a:
        copy.wait()
    for slot, mine in enumerate(copies_b):
        for copy in mine:
            copy.wait()
        z_part = z_lo if slot < X else 1 - z_lo
        block = z_part * X + lax.rem(x + slot % X, X)
        other = (block % Z_HI + z_hi) % 2
        place = other * Y + lax.rem(block // Z_HI - y + Y, Y)
        term = jnp.dot(left[place], right[slot], preferred_element_type=jnp.float32)
        if slot == 0:
            acc[...] = term
        elif slot < len(copies_b) - 1:
            acc[...] += term
        else:
            out_ref[...] = acc[...] + term


def local_product(a_groups, b_groups, rows, cols):
    counts_a, counts_b = [len(g) for g in a_groups], [len(g) for g in b_groups]
    parts = [p for g in a_groups for p in g] + [p for g in b_groups for p in g]
    slots = len(a_groups)
    depth = a_groups[0][0].shape[1]
    return pl.pallas_call(
        lambda *refs: product_kernel(counts_a, counts_b, *refs),
        out_shape=jax.ShapeDtypeStruct((rows, cols), jnp.float32),
        in_specs=[pl.BlockSpec(memory_space=pl.ANY)] * len(parts),
        out_specs=pl.BlockSpec(memory_space=pltpu.VMEM),
        scratch_shapes=[
            pltpu.VMEM((slots, rows, depth), jnp.bfloat16),
            pltpu.VMEM((slots, depth, cols), jnp.bfloat16),
            pltpu.VMEM((rows, cols), jnp.float32),
            pltpu.SemaphoreType.DMA((sum(counts_a),)),
            pltpu.SemaphoreType.DMA((sum(counts_b),)),
        ],
        compiler_params=pltpu.CompilerParams(vmem_limit_bytes=36 * 2**20),
        cost_estimate=pl.CostEstimate(
            flops=2 * rows * cols * depth * slots, bytes_accessed=20 * 2**20, transcendentals=0),
        name="local_product",
    )(*parts)


def encode(product):
    top = jnp.maximum(jnp.max(jnp.abs(product), axis=0, keepdims=True), 1e-30)
    power = jnp.ceil(jnp.log2(top) + 1e-3)
    coded = jnp.round(product * jnp.exp2(LEVELS - power)).astype(jnp.int16)
    return jnp.concatenate([coded, jnp.broadcast_to(power.astype(jnp.int16), (16, product.shape[1]))])


def decode(payload):
    power = payload[-1:].astype(jnp.float32)
    return payload[:-16].astype(jnp.float32) * jnp.exp2(power - LEVELS)


def shards(amplitudes, integrals, occ_energy, vir_energy, pair_occ, pair_vir):
    tile_rows, tile_cols = amplitudes.shape
    core = lax.axis_index("row") % CORE
    a_groups = gather(amplitudes, along_y, across_z_hi)
    b_groups = []
    for group in gather(integrals, along_x, across_z_lo):
        b_groups += [group, tuple(send(part, across_core) for part in group)]
    product = local_product(a_groups, b_groups, tile_rows, tile_cols)

    payload = encode(product)
    low, high = payload[:, :tile_rows], payload[:, tile_rows:]
    same = decode(send(jnp.where(core == 0, low, high), mirrored(0))).T
    cross = decode(send(jnp.where(core == 0, high, low), mirrored(1))).T
    mirror = jnp.concatenate([jnp.where(core == 0, same, cross), jnp.where(core == 0, cross, same)], axis=1)

    row_start = lax.axis_index("row") * tile_rows
    col_start = lax.axis_index("col") * tile_cols
    row_occ = lax.dynamic_slice_in_dim(pair_occ, row_start, tile_rows)
    row_vir = lax.dynamic_slice_in_dim(pair_vir, row_start, tile_rows)
    col_occ = lax.dynamic_slice_in_dim(pair_occ, col_start, tile_cols)
    col_vir = lax.dynamic_slice_in_dim(pair_vir, col_start, tile_cols)
    row_gap = lookup(occ_energy, row_occ) - lookup(vir_energy, row_vir)
    col_gap = lookup(occ_energy, col_occ) - lookup(vir_energy, col_vir)
    return (product + mirror) / (row_gap[:, None] + col_gap[None, :])


def solution(mesh):
    return jax.shard_map(
        shards,
        mesh=mesh,
        in_specs=(P("row", "col"), P("row", "col"), P(), P(), P(), P()),
        out_specs=P("row", "col"),
        check_vma=False,
    )
```

```python
import jax
import jax.numpy as jnp
from jax import lax
from jax.experimental import pallas as pl
from jax.experimental.pallas import tpu as pltpu
from jax.sharding import PartitionSpec as P

Z_LO, X, CORE, Y, Z_HI = 2, 4, 2, 4, 2
AXES = ("row", "col")
LEVELS = 15


def device_index(z_lo, x, core, y, z_hi):
    return ((z_lo * X + x) * CORE + core) * (Y * Z_HI) + y * Z_HI + z_hi


def places():
    for z_lo in range(Z_LO):
        for x in range(X):
            for core in range(CORE):
                for y in range(Y):
                    for z_hi in range(Z_HI):
                        yield z_lo, x, core, y, z_hi


def send(block, target):
    pairs = [(device_index(*place), device_index(*target(*place))) for place in places()]
    return lax.ppermute(block, AXES, pairs)


def along_y(step):
    return lambda z_lo, x, core, y, z_hi: (z_lo, x, core, (y + step) % Y, z_hi)


def across_z_hi(z_lo, x, core, y, z_hi):
    return z_lo, x, core, y, 1 - z_hi


def mirrored(flip):
    def target(z_lo, x, core, y, z_hi):
        chip_row, chip_col = z_lo * X + x, y * Z_HI + z_hi
        return chip_col // X, chip_col % X, core ^ flip, chip_row // Z_HI, chip_row % Z_HI

    return target


def ring(block, along):
    half = block.shape[0] // 2
    before = send(block, along(1))
    after = send(block, along(-1))
    top = send(before[:half], along(1))
    bottom = send(after[half:], along(-1))
    return [(block,), (after,), (top, bottom), (before,)]


def gather(block, along, across):
    return ring(block, along) + ring(send(block, across), along)


def lookup(energies, orbital_index):
    labels = jnp.arange(energies.shape[0], dtype=jnp.int32)
    picked = jnp.where(orbital_index[:, None] == labels[None, :], energies[None, :], 0.0)
    return jnp.sum(picked, axis=1)


def product_kernel(counts, first, *refs):
    parts, refs = refs[:sum(counts)], refs[sum(counts):]
    panel_ref, out_ref, same_ref, cross_ref, left, right, acc, sem_a, sem_b = refs
    row, col = lax.axis_index("row"), lax.axis_index("col")
    core, y, z_hi = row % CORE, col // Z_HI, col % Z_HI
    rows, depth = left.shape[1], left.shape[2]
    copies = []
    at = 0
    for slot, count in enumerate(counts):
        part = 2 * rows // count
        mine = []
        for i in range(count):
            low, high = max(i * part, first), min((i + 1) * part, first + rows)
            if low < high:
                mine.append(pltpu.make_async_copy(
                    parts[at].at[pl.ds(low - i * part, high - low), :],
                    left.at[slot, pl.ds(low - first, high - low), :], sem_a.at[at]))
            at += 1
        block = lax.rem(y + slot % Y, Y) * Z_HI + (z_hi if slot < Y else 1 - z_hi)
        mine.append(pltpu.make_async_copy(
            panel_ref.at[pl.ds(pl.multiple_of(block * depth, depth), depth), :],
            right.at[slot], sem_b.at[slot]))
        copies.append(mine)
    for mine in copies:
        for copy in mine:
            copy.start()
    for slot, mine in enumerate(copies):
        for copy in mine:
            copy.wait()
        term = jnp.dot(left[slot], right[slot], preferred_element_type=jnp.float32)
        if slot == 0:
            acc[...] = term
        elif slot < len(copies) - 1:
            acc[...] += term
        else:
            out_ref[...] = acc[...] + term
    half = out_ref.shape[1] // 2
    low, high = out_ref[:, :half], out_ref[:, half:]
    encode(jnp.where(core == 0, low, high), same_ref)
    encode(jnp.where(core == 0, high, low), cross_ref)


def encode(block, payload_ref):
    part = block.shape[0] // 2
    packed = jnp.concatenate([block[:part], block[part:]], axis=1)
    top = jnp.maximum(jnp.max(jnp.abs(packed), axis=0, keepdims=True), 1e-30)
    power = jnp.ceil(jnp.log2(top) + 1e-3)
    payload_ref[:part, :] = jnp.round(packed * jnp.exp2(LEVELS - power)).astype(jnp.int32).astype(jnp.int16)
    payload_ref[part:, :] = jnp.broadcast_to(power, (16, packed.shape[1])).astype(jnp.int32).astype(jnp.int16)


def decode(payload_ref):
    part = payload_ref.shape[0] - 16
    power = payload_ref[part:, :].astype(jnp.int32).astype(jnp.float32)[:1]
    packed = payload_ref[:part, :].astype(jnp.int32).astype(jnp.float32) * jnp.exp2(power - LEVELS)
    width = packed.shape[1] // 2
    return jnp.concatenate([packed[:, :width], packed[:, width:]])


def combine_kernel(*refs):
    *inputs, row_gap_ref, col_gap_ref, out_ref = refs
    count = len(inputs) // 3
    products, same, cross = inputs[:count], inputs[count:2 * count], inputs[2 * count:]
    core = lax.axis_index("row") % CORE
    same = jnp.concatenate([decode(p) for p in same]).T
    cross = jnp.concatenate([decode(p) for p in cross]).T
    mirror = jnp.concatenate(
        [jnp.where(core == 0, same, cross), jnp.where(core == 0, cross, same)], axis=1)
    at = 0
    for product in products:
        part = product.shape[0]
        gap = row_gap_ref[at:at + part, :] + col_gap_ref[...]
        out_ref[at:at + part, :] = (product[...] + mirror[at:at + part]) / gap
        at += part


def combine(products, same, cross, row_gap, col_gap):
    rows, cols = row_gap.shape[0], col_gap.shape[0]
    inputs = [*products, *same, *cross, row_gap[:, None], col_gap[None, :]]
    return pl.pallas_call(
        combine_kernel,
        out_shape=jax.ShapeDtypeStruct((rows, cols), jnp.float32),
        in_specs=[pl.BlockSpec(memory_space=pltpu.VMEM)] * len(inputs),
        out_specs=pl.BlockSpec(memory_space=pltpu.VMEM),
        compiler_params=pltpu.CompilerParams(vmem_limit_bytes=32 * 2**20),
        cost_estimate=pl.CostEstimate(flops=4 * rows * cols, bytes_accessed=12 * rows * cols, transcendentals=0),
        name="combine",
    )(*inputs)


def local_product(groups, panel, first, rows):
    counts = [len(g) for g in groups]
    parts = [p for g in groups for p in g]
    slots, depth, cols = len(groups), groups[0][0].shape[1], panel.shape[1]
    payload = jax.ShapeDtypeStruct((rows // 2 + 16, cols), jnp.int16)
    hbm = pl.BlockSpec(memory_space=pltpu.HBM)
    vmem = pl.BlockSpec(memory_space=pltpu.VMEM)
    return pl.pallas_call(
        lambda *refs: product_kernel(counts, first, *refs),
        out_shape=[jax.ShapeDtypeStruct((rows, cols), jnp.float32), payload, payload],
        in_specs=[hbm] * (len(parts) + 1),
        out_specs=[vmem] * 3,
        scratch_shapes=[
            pltpu.VMEM((slots, rows, depth), jnp.bfloat16),
            pltpu.VMEM((slots, depth, cols), jnp.bfloat16),
            pltpu.VMEM((rows, cols), jnp.float32),
            pltpu.SemaphoreType.DMA((len(parts),)),
            pltpu.SemaphoreType.DMA((slots,)),
        ],
        compiler_params=pltpu.CompilerParams(vmem_limit_bytes=60 * 2**20),
        cost_estimate=pl.CostEstimate(
            flops=2 * rows * cols * depth * slots, bytes_accessed=16 * 2**20, transcendentals=0),
        name="local_product",
    )(*parts, panel)


def shards(amplitudes, integrals, occ_energy, vir_energy, pair_occ, pair_vir):
    tile_rows, tile_cols = amplitudes.shape
    panel = lax.all_gather(integrals, "row", axis=0, tiled=True)
    groups = gather(amplitudes, along_y, across_z_hi)
    part = tile_rows // 2
    products, same, cross = [], [], []
    for first in (0, part):
        product, to_same, to_cross = local_product(groups, panel, first, part)
        products.append(product)
        same.append(send(to_same, mirrored(0)))
        cross.append(send(to_cross, mirrored(1)))
    row_start = lax.axis_index("row") * tile_rows
    col_start = lax.axis_index("col") * tile_cols
    row_occ = lax.dynamic_slice_in_dim(pair_occ, row_start, tile_rows)
    row_vir = lax.dynamic_slice_in_dim(pair_vir, row_start, tile_rows)
    col_occ = lax.dynamic_slice_in_dim(pair_occ, col_start, tile_cols)
    col_vir = lax.dynamic_slice_in_dim(pair_vir, col_start, tile_cols)
    row_gap = lookup(occ_energy, row_occ) - lookup(vir_energy, row_vir)
    col_gap = lookup(occ_energy, col_occ) - lookup(vir_energy, col_vir)
    return combine(products, same, cross, row_gap, col_gap)


def solution(mesh):
    return jax.shard_map(
        shards,
        mesh=mesh,
        in_specs=(P("row", "col"), P("row", "col"), P(), P(), P(), P()),
        out_specs=P("row", "col"),
        check_vma=False,
    )
```

```python
import jax
import jax.numpy as jnp
from jax import lax
from jax.experimental import pallas as pl
from jax.experimental.pallas import tpu as pltpu
from jax.sharding import PartitionSpec as P

Z_LO, X, CORE, Y, Z_HI = 2, 4, 2, 4, 2
AXES = ("row", "col")
LEVELS = 15
MIB = 2**20


def device_index(z_lo, x, core, y, z_hi):
    return ((z_lo * X + x) * CORE + core) * (Y * Z_HI) + y * Z_HI + z_hi


def places():
    for z_lo in range(Z_LO):
        for x in range(X):
            for core in range(CORE):
                for y in range(Y):
                    for z_hi in range(Z_HI):
                        yield z_lo, x, core, y, z_hi


def send(block, target):
    pairs = [(device_index(*place), device_index(*target(*place))) for place in places()]
    return lax.ppermute(block, AXES, pairs)


def along_x(step):
    return lambda z_lo, x, core, y, z_hi: (z_lo, (x + step) % X, core, y, z_hi)


def along_y(step):
    return lambda z_lo, x, core, y, z_hi: (z_lo, x, core, (y + step) % Y, z_hi)


def across_z_lo(z_lo, x, core, y, z_hi):
    return 1 - z_lo, x, core, y, z_hi


def across_z_hi(z_lo, x, core, y, z_hi):
    return z_lo, x, core, y, 1 - z_hi


def across_core(z_lo, x, core, y, z_hi):
    return z_lo, x, 1 - core, y, z_hi


def mirrored(flip):
    def target(z_lo, x, core, y, z_hi):
        chip_row, chip_col = z_lo * X + x, y * Z_HI + z_hi
        return chip_col // X, chip_col % X, core ^ flip, chip_row // Z_HI, chip_row % Z_HI

    return target


def after(block, *earlier):
    return lax.optimization_barrier((block, *earlier))[0]


def gather(left, right):
    half = left.shape[0] // 2
    right_z = send(right, across_z_lo)
    right_up, right_down = send(right, along_x(1)), send(right, along_x(-1))
    left_up, left_down = send(left, along_y(1)), send(left, along_y(-1))
    left_z = send(after(left, right_z), across_z_hi)
    right_z = after(right_z, right_up, right_down)
    right_z_up, right_z_down = send(right_z, along_x(1)), send(right_z, along_x(-1))
    left_top, left_bottom = send(left_up[:half], along_y(1)), send(left_down[half:], along_y(-1))
    left_z_up, left_z_down = send(left_z, along_y(1)), send(left_z, along_y(-1))
    right_top = send(jnp.concatenate([right_up[:half], right_z_up[:half]]), along_x(1))
    right_bottom = send(jnp.concatenate([right_down[half:], right_z_down[half:]]), along_x(-1))
    left_z_top, left_z_bottom = send(left_z_up[:half], along_y(1)), send(left_z_down[half:], along_y(-1))
    near = [(left, 0, 0), (left_down, 1, 0), (left_top, 2, 0), (left_bottom, 2, half), (left_up, 3, 0)]
    far = [(left_z, 0, 0), (left_z_down, 1, 0), (left_z_top, 2, 0), (left_z_bottom, 2, half), (left_z_up, 3, 0)]
    return near, far, [
        (right, 0), (right_down, 1), (right_up, 3), (right_z, 4), (right_z_down, 5), (right_z_up, 7),
        (right_top, 2, 6), (right_bottom, 2, 6)]


def lookup(energies, orbital_index):
    labels = jnp.arange(energies.shape[0], dtype=jnp.int32)
    picked = jnp.where(orbital_index[:, None] == labels[None, :], energies[None, :], 0.0)
    return jnp.sum(picked, axis=1)


def partial_kernel(far, left_places, right_places, *refs):
    left_parts, refs = refs[:len(left_places)], refs[len(left_places):]
    right_parts, refs = refs[:len(right_places)], refs[len(right_places):]
    if far:
        sum_ref, give_ref, keep_ref, left, right, acc, sem_left, sem_right = refs
    else:
        out_ref, left, right, acc, sem_left, sem_right = refs
    row, col = lax.axis_index("row"), lax.axis_index("col")
    z_lo, x, core = row // (X * CORE), (row // CORE) % X, row % CORE
    y, z_hi = col // Z_HI, col % Z_HI
    rows, depth = left.shape[1], left.shape[2] // 2
    half = rows // 2
    copies = []
    for i, (slot, at) in enumerate(left_places):
        part = left_parts[i]
        copies.append(pltpu.make_async_copy(part, left.at[slot, pl.ds(at, part.shape[0]), :], sem_left.at[i]))
    at = 0
    for i, (first, *second) in enumerate(right_places):
        part = right_parts[i]
        if second:
            base = half if i == len(right_places) - 1 else 0
            for which, slot in enumerate((first, *second)):
                copies.append(pltpu.make_async_copy(
                    part.at[pl.ds(which * half, half), :], right.at[slot, pl.ds(base, half), :], sem_right.at[at]))
                at += 1
        else:
            copies.append(pltpu.make_async_copy(part, right.at[first], sem_right.at[at]))
            at += 1
    for copy in copies:
        copy.start()
    for copy in copies:
        copy.wait()
    for slot in range(Y):
        block = lax.rem(y + slot, Y) * Z_HI + (1 - z_hi if far else z_hi)
        plane = (block // X + z_lo) % Z_LO
        place = plane * X + lax.rem(block % X - x + X, X)
        both = jnp.concatenate([left[slot][:, :depth], left[slot][:, depth:]])
        term = jnp.dot(both, right[place], preferred_element_type=jnp.float32)
        if slot == 0:
            acc[...] = term + sum_ref[...] if far else term
        elif far or slot < Y - 1:
            acc[...] += term
        else:
            out_ref[...] = acc[...] + term
    if far:
        give_ref[...] = acc[pl.ds(pl.multiple_of((1 - core) * rows, rows), rows), :]
        keep_ref[...] = acc[pl.ds(pl.multiple_of(core * rows, rows), rows), :]


def partial_product(left, right, earlier=None):
    far = earlier is not None
    rows, cols = left[0][0].shape
    parts = [part for part, *_ in left] + [part for part, *_ in right] + ([earlier] if far else [])
    left_places = [tuple(place) for _, *place in left]
    right_places = [tuple(place) for _, *place in right]
    whole = jax.ShapeDtypeStruct((2 * rows, cols), jnp.float32)
    one = jax.ShapeDtypeStruct((rows, cols), jnp.float32)
    vmem = pl.BlockSpec(memory_space=pltpu.VMEM)
    return pl.pallas_call(
        lambda *refs: partial_kernel(far, left_places, right_places, *refs),
        out_shape=[one, one] if far else whole,
        in_specs=[pl.BlockSpec(memory_space=pl.ANY)] * (len(left) + len(right)) + ([vmem] if far else []),
        out_specs=[vmem, vmem] if far else vmem,
        scratch_shapes=[
            pltpu.VMEM((Y, rows, cols), jnp.bfloat16),
            pltpu.VMEM((Z_LO * X, rows, cols), jnp.bfloat16),
            pltpu.VMEM((2 * rows, cols), jnp.float32),
            pltpu.SemaphoreType.DMA((len(left),)),
            pltpu.SemaphoreType.DMA((len(right) + 2,)),
        ],
        compiler_params=pltpu.CompilerParams(vmem_limit_bytes=26 * MIB),
        cost_estimate=pl.CostEstimate(
            flops=2 * Y * 2 * rows * cols * cols // 2, bytes_accessed=18 * MIB, transcendentals=0),
        name="partial_product",
    )(*parts)


def encode(block, payload_ref):
    part = block.shape[0] // 2
    packed = jnp.concatenate([block[:part], block[part:]], axis=1)
    top = jnp.maximum(jnp.max(jnp.abs(packed), axis=0, keepdims=True), 1e-30)
    power = jnp.ceil(jnp.log2(top) + 1e-3)
    payload_ref[:part, :] = jnp.round(packed * jnp.exp2(LEVELS - power)).astype(jnp.int32).astype(jnp.int16)
    payload_ref[part:, :] = jnp.broadcast_to(power, (16, packed.shape[1])).astype(jnp.int32).astype(jnp.int16)


def decode(payload_ref):
    part = payload_ref.shape[0] - 16
    power = payload_ref[part:, :].astype(jnp.int32).astype(jnp.float32)[:1]
    packed = payload_ref[:part, :].astype(jnp.int32).astype(jnp.float32) * jnp.exp2(power - LEVELS)
    width = packed.shape[1] // 2
    return jnp.concatenate([packed[:, :width], packed[:, width:]])


def join_kernel(keep_ref, got_ref, out_ref, same_ref, cross_ref):
    core = lax.axis_index("row") % CORE
    out_ref[...] = keep_ref[...] + got_ref[...]
    half = out_ref.shape[1] // 2
    low, high = out_ref[:, :half], out_ref[:, half:]
    encode(jnp.where(core == 0, low, high), same_ref)
    encode(jnp.where(core == 0, high, low), cross_ref)


def join(keep, got):
    rows, cols = keep.shape
    payload = jax.ShapeDtypeStruct((rows // 2 + 16, cols), jnp.int16)
    vmem = pl.BlockSpec(memory_space=pltpu.VMEM)
    return pl.pallas_call(
        join_kernel,
        out_shape=[jax.ShapeDtypeStruct((rows, cols), jnp.float32), payload, payload],
        in_specs=[vmem] * 2,
        out_specs=[vmem] * 3,
        compiler_params=pltpu.CompilerParams(vmem_limit_bytes=26 * MIB),
        cost_estimate=pl.CostEstimate(flops=4 * rows * cols, bytes_accessed=12 * rows * cols, transcendentals=0),
        name="join",
    )(keep, got)


def combine_kernel(product_ref, same_ref, cross_ref, row_gap_ref, col_gap_ref, out_ref):
    core = lax.axis_index("row") % CORE
    same, cross = decode(same_ref).T, decode(cross_ref).T
    mirror = jnp.concatenate(
        [jnp.where(core == 0, same, cross), jnp.where(core == 0, cross, same)], axis=1)
    out_ref[...] = (product_ref[...] + mirror) / (row_gap_ref[...] + col_gap_ref[...])


def combine(product, same, cross, row_gap, col_gap):
    rows, cols = product.shape
    return pl.pallas_call(
        combine_kernel,
        out_shape=jax.ShapeDtypeStruct((rows, cols), jnp.float32),
        in_specs=[pl.BlockSpec(memory_space=pltpu.VMEM)] * 5,
        out_specs=pl.BlockSpec(memory_space=pltpu.VMEM),
        compiler_params=pltpu.CompilerParams(vmem_limit_bytes=26 * MIB),
        cost_estimate=pl.CostEstimate(flops=4 * rows * cols, bytes_accessed=12 * rows * cols, transcendentals=0),
        name="combine",
    )(product, same, cross, row_gap[:, None], col_gap[None, :])


def shards(amplitudes, integrals, occ_energy, vir_energy, pair_occ, pair_vir):
    tile_rows, tile_cols = amplitudes.shape
    core = lax.axis_index("row") % CORE
    other = send(jnp.roll(amplitudes, tile_cols // 2, axis=1), across_core)
    lane = lax.broadcasted_iota(jnp.int32, amplitudes.shape, 1)
    left = jnp.where((lane < tile_cols // 2) == (core == 0), amplitudes, other)
    near, far, right = gather(left, integrals)
    give, keep = partial_product(far, right, partial_product(near, right))
    product, to_same, to_cross = join(keep, send(give, across_core))
    same, cross = send(to_same, mirrored(0)), send(to_cross, mirrored(1))

    row_start = lax.axis_index("row") * tile_rows
    col_start = lax.axis_index("col") * tile_cols
    row_occ = lax.dynamic_slice_in_dim(pair_occ, row_start, tile_rows)
    row_vir = lax.dynamic_slice_in_dim(pair_vir, row_start, tile_rows)
    col_occ = lax.dynamic_slice_in_dim(pair_occ, col_start, tile_cols)
    col_vir = lax.dynamic_slice_in_dim(pair_vir, col_start, tile_cols)
    row_gap = lookup(occ_energy, row_occ) - lookup(vir_energy, row_vir)
    col_gap = lookup(occ_energy, col_occ) - lookup(vir_energy, col_vir)
    return combine(product, same, cross, row_gap, col_gap)


def solution(mesh):
    return jax.shard_map(
        shards,
        mesh=mesh,
        in_specs=(P("row", "col"), P("row", "col"), P(), P(), P(), P()),
        out_specs=P("row", "col"),
        check_vma=False,
    )
```

```python
import jax
import jax.numpy as jnp
from jax import lax
from jax.experimental import pallas as pl
from jax.experimental.pallas import tpu as pltpu
from jax.sharding import PartitionSpec as P

Z_LO, X, CORE, Y, Z_HI = 2, 4, 2, 4, 2
AXES = ("row", "col")
LEVELS = 15
MIB = 2**20


def device_index(z_lo, x, core, y, z_hi):
    return ((z_lo * X + x) * CORE + core) * (Y * Z_HI) + y * Z_HI + z_hi


def places():
    for z_lo in range(Z_LO):
        for x in range(X):
            for core in range(CORE):
                for y in range(Y):
                    for z_hi in range(Z_HI):
                        yield z_lo, x, core, y, z_hi


def send(block, target):
    pairs = [(device_index(*place), device_index(*target(*place))) for place in places()]
    return lax.ppermute(block, AXES, pairs)


def along_x(step):
    return lambda z_lo, x, core, y, z_hi: (z_lo, (x + step) % X, core, y, z_hi)


def along_y(step):
    return lambda z_lo, x, core, y, z_hi: (z_lo, x, core, (y + step) % Y, z_hi)


def across_z_lo(z_lo, x, core, y, z_hi):
    return 1 - z_lo, x, core, y, z_hi


def across_z_hi(z_lo, x, core, y, z_hi):
    return z_lo, x, core, y, 1 - z_hi


def across_core(z_lo, x, core, y, z_hi):
    return z_lo, x, 1 - core, y, z_hi


def mirrored(flip):
    def target(z_lo, x, core, y, z_hi):
        chip_row, chip_col = z_lo * X + x, y * Z_HI + z_hi
        return chip_col // X, chip_col % X, core ^ flip, chip_row // Z_HI, chip_row % Z_HI

    return target


def detour(z_lo, x, core, y, z_hi):
    x_bit = x // 2 ^ y % 2 ^ z_hi
    return x % 2 ^ z_hi ^ z_lo, x // 2 * 2 + x_bit, core, y, x % 2


def after_detour(z_lo, x, core, y, z_hi):
    start = next(place for place in places() if detour(*place) == (z_lo, x, core, y, z_hi))
    return mirrored(1)(*start)


def after(block, *earlier):
    return lax.optimization_barrier((block, *earlier))[0]


def gather(left, right):
    half = left.shape[0] // 2
    right_z = send(right, across_z_lo)
    right_up, right_down = send(right, along_x(1)), send(right, along_x(-1))
    left_up, left_down = send(left, along_y(1)), send(left, along_y(-1))
    left_z = send(after(left, right_z), across_z_hi)
    right_z = after(right_z, right_up, right_down)
    right_z_up, right_z_down = send(right_z, along_x(1)), send(right_z, along_x(-1))
    left_top, left_bottom = send(left_up[:half], along_y(1)), send(left_down[half:], along_y(-1))
    left_z = after(left_z, left_top, left_bottom)
    left_z_up, left_z_down = send(left_z, along_y(1)), send(left_z, along_y(-1))
    right_top = send(jnp.concatenate([right_up[:half], right_z_up[:half]]), along_x(1))
    right_bottom = send(jnp.concatenate([right_down[half:], right_z_down[half:]]), along_x(-1))
    left_z_top, left_z_bottom = send(left_z_up[:half], along_y(1)), send(left_z_down[half:], along_y(-1))
    near = [(left,), (left_down,), (left_top, left_bottom), (left_up,)]
    far = [(left_z,), (left_z_down,), (left_z_top, left_z_bottom), (left_z_up,)]
    return near, far, [
        (right, 0), (right_down, 1), (right_up, 3), (right_z, 4), (right_z_down, 5), (right_z_up, 7),
        (right_top, 2, 6), (right_bottom, 2, 6)]


def lookup(energies, orbital_index):
    labels = jnp.arange(energies.shape[0], dtype=jnp.int32)
    picked = jnp.where(orbital_index[:, None] == labels[None, :], energies[None, :], 0.0)
    return jnp.sum(picked, axis=1)


def whole(parts, lanes):
    return jnp.concatenate([part[:, lanes] for part in parts]) if len(parts) > 1 else parts[0][:, lanes]


def grouped(refs, counts):
    groups, at = [], 0
    for count in counts:
        groups.append(refs[at:at + count])
        at += count
    return groups, refs[at:]


def place_of(slot, far):
    row, col = lax.axis_index("row"), lax.axis_index("col")
    z_lo, x = row // (X * CORE), (row // CORE) % X
    y, z_hi = col // Z_HI, col % Z_HI
    block = lax.rem(y + slot, Y) * Z_HI + (1 - z_hi if far else z_hi)
    return (block // X + z_lo) % Z_LO * X + lax.rem(block % X - x + X, X)


def near_kernel(counts, right_places, *refs):
    left, refs = grouped(refs, counts)
    right_parts, (sum_ref, stack_ref, acc, sem) = refs[:len(right_places)], refs[len(right_places):]
    rows, depth = stack_ref.shape[1], stack_ref.shape[2] // 2
    half = rows // 2
    copies = []
    for i, (first, *second) in enumerate(right_places):
        part = right_parts[i]
        if second:
            base = half if i == len(right_places) - 1 else 0
            for which, slot in enumerate((first, *second)):
                copies.append(pltpu.make_async_copy(
                    part.at[pl.ds(which * half, half), :], stack_ref.at[slot, pl.ds(base, half), :],
                    sem.at[len(copies)]))
        else:
            copies.append(pltpu.make_async_copy(part, stack_ref.at[first], sem.at[len(copies)]))
    for copy in copies:
        copy.start()
    for copy in copies:
        copy.wait()
    for slot in range(Y):
        both = jnp.concatenate([whole(left[slot], slice(0, depth)), whole(left[slot], slice(depth, 2 * depth))])
        term = jnp.dot(both, stack_ref[place_of(slot, False)], preferred_element_type=jnp.float32)
        if slot == 0:
            acc[...] = term
        elif slot < Y - 1:
            acc[...] += term
        else:
            sum_ref[...] = acc[...] + term


def near_product(left, right):
    rows, cols = left[0][0].shape
    counts = [len(group) for group in left]
    right_places = [tuple(place) for _, *place in right]
    vmem = pl.BlockSpec(memory_space=pltpu.VMEM)
    return pl.pallas_call(
        lambda *refs: near_kernel(counts, right_places, *refs),
        out_shape=[
            jax.ShapeDtypeStruct((2 * rows, cols), jnp.float32),
            jax.ShapeDtypeStruct((Z_LO * X, rows, cols), jnp.bfloat16)],
        in_specs=[vmem] * sum(counts) + [pl.BlockSpec(memory_space=pl.ANY)] * len(right),
        out_specs=[vmem] * 2,
        scratch_shapes=[
            pltpu.VMEM((2 * rows, cols), jnp.float32),
            pltpu.SemaphoreType.DMA((len(right) + 2,)),
        ],
        compiler_params=pltpu.CompilerParams(vmem_limit_bytes=24 * MIB),
        cost_estimate=pl.CostEstimate(
            flops=4 * Y * rows * cols * cols // 2, bytes_accessed=18 * MIB, transcendentals=0),
        name="near_product",
    )(*[part for group in left for part in group], *[part for part, *_ in right])


def far_kernel(counts, own, *refs):
    left, (sum_ref, stack_ref, out_ref, acc) = grouped(refs, counts)
    depth = stack_ref.shape[2] // 2
    rows = out_ref.shape[0]
    first = 0 if own else 1
    lanes = slice(first * depth, (first + 1) * depth)
    for slot in range(Y):
        term = jnp.dot(
            whole(left[slot], lanes), stack_ref[place_of(slot, True)], preferred_element_type=jnp.float32)
        if slot == 0:
            acc[...] = term + sum_ref[first * rows:(first + 1) * rows, :]
        elif slot < Y - 1:
            acc[...] += term
        else:
            out_ref[...] = acc[...] + term


def far_product(left, total, stack, own):
    rows, cols = left[0][0].shape
    counts = [len(group) for group in left]
    vmem = pl.BlockSpec(memory_space=pltpu.VMEM)
    return pl.pallas_call(
        lambda *refs: far_kernel(counts, own, *refs),
        out_shape=jax.ShapeDtypeStruct((rows, cols), jnp.float32),
        in_specs=[vmem] * (sum(counts) + 2),
        out_specs=vmem,
        scratch_shapes=[pltpu.VMEM((rows, cols), jnp.float32)],
        compiler_params=pltpu.CompilerParams(vmem_limit_bytes=24 * MIB),
        cost_estimate=pl.CostEstimate(
            flops=2 * Y * rows * cols * cols // 2, bytes_accessed=12 * MIB, transcendentals=0),
        name="far_product",
    )(*[part for group in left for part in group], total, stack)


def encode(block, payload_ref):
    part = block.shape[0] // 2
    packed = jnp.concatenate([block[:part], block[part:]], axis=1)
    top = jnp.maximum(jnp.max(jnp.abs(packed), axis=0, keepdims=True), 1e-30)
    power = jnp.ceil(jnp.log2(top) + 1e-3)
    payload_ref[:part, :] = jnp.round(packed * jnp.exp2(LEVELS - power)).astype(jnp.int32).astype(jnp.int16)
    payload_ref[part:, :] = jnp.broadcast_to(power, (16, packed.shape[1])).astype(jnp.int32).astype(jnp.int16)


def decode(payload_ref):
    part = payload_ref.shape[0] - 16
    power = payload_ref[part:, :].astype(jnp.int32).astype(jnp.float32)[:1]
    packed = payload_ref[:part, :].astype(jnp.int32).astype(jnp.float32) * jnp.exp2(power - LEVELS)
    width = packed.shape[1] // 2
    return jnp.concatenate([packed[:, :width], packed[:, width:]])


def join_kernel(keep_ref, got_ref, out_ref, same_ref, cross_ref):
    core = lax.axis_index("row") % CORE
    out_ref[...] = keep_ref[...] + got_ref[...]
    half = out_ref.shape[1] // 2
    low, high = out_ref[:, :half], out_ref[:, half:]
    encode(jnp.where(core == 0, low, high), same_ref)
    encode(jnp.where(core == 0, high, low), cross_ref)


def join(keep, got):
    rows, cols = keep.shape
    payload = jax.ShapeDtypeStruct((rows // 2 + 16, cols), jnp.int16)
    vmem = pl.BlockSpec(memory_space=pltpu.VMEM)
    return pl.pallas_call(
        join_kernel,
        out_shape=[jax.ShapeDtypeStruct((rows, cols), jnp.float32), payload, payload],
        in_specs=[vmem] * 2,
        out_specs=[vmem] * 3,
        compiler_params=pltpu.CompilerParams(vmem_limit_bytes=16 * MIB),
        cost_estimate=pl.CostEstimate(flops=4 * rows * cols, bytes_accessed=12 * rows * cols, transcendentals=0),
        name="join",
    )(keep, got)


def combine_kernel(product_ref, same_ref, cross_ref, row_gap_ref, col_gap_ref, out_ref):
    core = lax.axis_index("row") % CORE
    same, cross = decode(same_ref).T, decode(cross_ref).T
    mirror = jnp.concatenate(
        [jnp.where(core == 0, same, cross), jnp.where(core == 0, cross, same)], axis=1)
    out_ref[...] = (product_ref[...] + mirror) / (row_gap_ref[...] + col_gap_ref[...])


def combine(product, same, cross, row_gap, col_gap):
    rows, cols = product.shape
    return pl.pallas_call(
        combine_kernel,
        out_shape=jax.ShapeDtypeStruct((rows, cols), jnp.float32),
        in_specs=[pl.BlockSpec(memory_space=pltpu.VMEM)] * 5,
        out_specs=pl.BlockSpec(memory_space=pltpu.VMEM),
        compiler_params=pltpu.CompilerParams(vmem_limit_bytes=26 * MIB),
        cost_estimate=pl.CostEstimate(flops=4 * rows * cols, bytes_accessed=12 * rows * cols, transcendentals=0),
        name="combine",
    )(product, same, cross, row_gap[:, None], col_gap[None, :])


def shards(amplitudes, integrals, occ_energy, vir_energy, pair_occ, pair_vir):
    tile_rows, tile_cols = amplitudes.shape
    core = lax.axis_index("row") % CORE
    other = send(amplitudes, across_core)
    lane = lax.broadcasted_iota(jnp.int32, amplitudes.shape, 1)
    half = tile_cols // 2
    left = jnp.where(
        lane < half,
        jnp.where(core == 0, amplitudes, jnp.roll(amplitudes, half, axis=1)),
        jnp.where(core == 0, jnp.roll(other, half, axis=1), other))
    near, far, right = gather(left, integrals)
    total, stack = near_product(near, right)
    give = far_product(far, total, stack, False)
    got = send(give, across_core)
    keep = far_product(far, total, stack, True)
    product, to_same, to_cross = join(keep, got)
    same = send(to_same, mirrored(0))
    cross = send(send(to_cross, detour), after_detour)

    row_start = lax.axis_index("row") * tile_rows
    col_start = lax.axis_index("col") * tile_cols
    row_occ = lax.dynamic_slice_in_dim(pair_occ, row_start, tile_rows)
    row_vir = lax.dynamic_slice_in_dim(pair_vir, row_start, tile_rows)
    col_occ = lax.dynamic_slice_in_dim(pair_occ, col_start, tile_cols)
    col_vir = lax.dynamic_slice_in_dim(pair_vir, col_start, tile_cols)
    row_gap = lookup(occ_energy, row_occ) - lookup(vir_energy, row_vir)
    col_gap = lookup(occ_energy, col_occ) - lookup(vir_energy, col_vir)
    return combine(product, same, cross, row_gap, col_gap)


def solution(mesh):
    return jax.shard_map(
        shards,
        mesh=mesh,
        in_specs=(P("row", "col"), P("row", "col"), P(), P(), P(), P()),
        out_specs=P("row", "col"),
        check_vma=False,
    )
```

```python
import jax
import jax.numpy as jnp
from jax import lax
from jax.experimental import pallas as pl
from jax.experimental.pallas import tpu as pltpu
from jax.sharding import PartitionSpec as P

Z_LO, X, CORE, Y, Z_HI = 2, 4, 2, 4, 2
AXES = ("row", "col")
LEVELS = 15
MIB = 2**20


def device_index(z_lo, x, core, y, z_hi):
    return ((z_lo * X + x) * CORE + core) * (Y * Z_HI) + y * Z_HI + z_hi


def places():
    for z_lo in range(Z_LO):
        for x in range(X):
            for core in range(CORE):
                for y in range(Y):
                    for z_hi in range(Z_HI):
                        yield z_lo, x, core, y, z_hi


def send(block, target):
    pairs = [(device_index(*place), device_index(*target(*place))) for place in places()]
    return lax.ppermute(block, AXES, pairs)


def along_x(step):
    return lambda z_lo, x, core, y, z_hi: (z_lo, (x + step) % X, core, y, z_hi)


def along_y(step):
    return lambda z_lo, x, core, y, z_hi: (z_lo, x, core, (y + step) % Y, z_hi)


def across_z_lo(z_lo, x, core, y, z_hi):
    return 1 - z_lo, x, core, y, z_hi


def across_z_hi(z_lo, x, core, y, z_hi):
    return z_lo, x, core, y, 1 - z_hi


def across_core(z_lo, x, core, y, z_hi):
    return z_lo, x, 1 - core, y, z_hi


def mirrored(flip):
    def target(z_lo, x, core, y, z_hi):
        chip_row, chip_col = z_lo * X + x, y * Z_HI + z_hi
        return chip_col // X, chip_col % X, core ^ flip, chip_row // Z_HI, chip_row % Z_HI

    return target


def detour(z_lo, x, core, y, z_hi):
    x_bit = x // 2 ^ y % 2 ^ z_hi
    return x % 2 ^ z_hi ^ z_lo, x // 2 * 2 + x_bit, core, y, x % 2


def after_detour(z_lo, x, core, y, z_hi):
    start = next(place for place in places() if detour(*place) == (z_lo, x, core, y, z_hi))
    return mirrored(1)(*start)


def after(block, *earlier):
    return lax.optimization_barrier((block, *earlier))[0]


def gather(left, right, other):
    half = left.shape[0] // 2
    right_z = send(right, across_z_lo)
    late = after(right, other)
    right_up, right_down = send(late, along_x(1)), send(late, along_x(-1))
    left_up, left_down = send(left, along_y(1)), send(left, along_y(-1))
    left_z = send(after(left, right_z), across_z_hi)
    right_up, right_down, right_z = lax.optimization_barrier((right_up, right_down, right_z))
    right_two = send(right_up, along_x(1))
    right_z_down = send(right_z, along_x(-1))
    right_z_up = send(after(right_z, right_two), along_x(1))
    right_z_two = send(right_z_down, along_x(-1))
    left_two = jnp.concatenate([send(left_up[:half], along_y(1)), send(left_down[half:], along_y(-1))])
    left_z, left_two = lax.optimization_barrier((left_z, left_two))
    left_z_up, left_z_down = send(left_z, along_y(1)), send(left_z, along_y(-1))
    left_z_two = send(left_two, across_z_hi)
    near = [left, left_down, left_two, left_up]
    far = [left_z, left_z_down, left_z_two, left_z_up]
    return near, far, [right, right_down, right_two, right_up, right_z, right_z_down], [right_z_two, right_z_up]


def block_of(values, index, count):
    table = values.reshape(count, -1)
    rows = lax.broadcasted_iota(jnp.int32, table.shape, 0)
    return jnp.sum(jnp.where(rows == index, table, 0), axis=0)


def lookup(energies, orbital_index):
    labels = jnp.arange(energies.shape[0], dtype=jnp.int32)
    picked = jnp.where(orbital_index[:, None] == labels[None, :], energies[None, :], 0.0)
    return jnp.sum(picked, axis=1)


LATE = 2


def stack_kernel(*refs):
    *parts, stack_ref, sem = refs
    copies = [pltpu.make_async_copy(part, stack_ref.at[i], sem.at[i]) for i, part in enumerate(parts)]
    for copy in copies:
        copy.start()
    for copy in copies:
        copy.wait()


def stacked(parts):
    rows, cols = parts[0].shape
    return pl.pallas_call(
        stack_kernel,
        out_shape=jax.ShapeDtypeStruct((len(parts) + LATE, rows, cols), jnp.bfloat16),
        in_specs=[pl.BlockSpec(memory_space=pl.ANY)] * len(parts),
        out_specs=pl.BlockSpec(memory_space=pltpu.VMEM),
        scratch_shapes=[pltpu.SemaphoreType.DMA((len(parts),))],
        compiler_params=pltpu.CompilerParams(vmem_limit_bytes=4 * MIB),
        cost_estimate=pl.CostEstimate(flops=0, bytes_accessed=4 * MIB, transcendentals=0),
        name="stacked",
    )(*parts)


def place_of(slot, far):
    row, col = lax.axis_index("row"), lax.axis_index("col")
    z_lo, x = row // (X * CORE), (row // CORE) % X
    y, z_hi = col // Z_HI, col % Z_HI
    block = lax.rem(y + slot, Y) * Z_HI + (1 - z_hi if far else z_hi)
    return (block // X + z_lo) % Z_LO * X + lax.rem(block % X - x + X, X)


def near_kernel(*refs):
    left, late, (_, sum_ref, stack_ref, acc, sem) = refs[:Y], refs[Y:Y + LATE], refs[Y + LATE:]
    depth = stack_ref.shape[2] // 2
    first = stack_ref.shape[0] - LATE
    copies = [pltpu.make_async_copy(part, stack_ref.at[first + i], sem.at[i]) for i, part in enumerate(late)]
    for copy in copies:
        copy.start()
    for copy in copies:
        copy.wait()
    for slot in range(Y):
        both = jnp.concatenate([left[slot][:, :depth], left[slot][:, depth:]])
        term = jnp.dot(both, stack_ref[place_of(slot, False)], preferred_element_type=jnp.float32)
        if slot == 0:
            acc[...] = term
        elif slot < Y - 1:
            acc[...] += term
        else:
            sum_ref[...] = acc[...] + term


def near_product(left, right, stack):
    rows, cols = left[0].shape
    vmem = pl.BlockSpec(memory_space=pltpu.VMEM)
    return pl.pallas_call(
        near_kernel,
        out_shape=[
            jax.ShapeDtypeStruct((2 * rows, cols), jnp.float32),
            jax.ShapeDtypeStruct(stack.shape, stack.dtype)],
        in_specs=[vmem] * Y + [pl.BlockSpec(memory_space=pl.ANY)] * LATE + [vmem],
        out_specs=[vmem] * 2,
        scratch_shapes=[
            pltpu.VMEM((2 * rows, cols), jnp.float32),
            pltpu.SemaphoreType.DMA((LATE,)),
        ],
        input_output_aliases={Y + LATE: 1},
        compiler_params=pltpu.CompilerParams(vmem_limit_bytes=10 * MIB),
        cost_estimate=pl.CostEstimate(
            flops=4 * Y * rows * cols * cols // 2, bytes_accessed=12 * MIB, transcendentals=0),
        name="near_product",
    )(*left, *right, stack)


def far_kernel(own, *refs):
    left, (sum_ref, stack_ref, out_ref, acc) = refs[:Y], refs[Y:]
    depth = stack_ref.shape[2] // 2
    rows = out_ref.shape[0]
    first = 0 if own else 1
    for slot in range(Y):
        term = jnp.dot(
            left[slot][:, first * depth:(first + 1) * depth], stack_ref[place_of(slot, True)],
            preferred_element_type=jnp.float32)
        if slot == 0:
            acc[...] = term + sum_ref[first * rows:(first + 1) * rows, :]
        elif slot < Y - 1:
            acc[...] += term
        else:
            out_ref[...] = acc[...] + term


def far_product(left, total, stack, own):
    rows, cols = left[0].shape
    vmem = pl.BlockSpec(memory_space=pltpu.VMEM)
    return pl.pallas_call(
        lambda *refs: far_kernel(own, *refs),
        out_shape=jax.ShapeDtypeStruct((rows, cols), jnp.float32),
        in_specs=[vmem] * (Y + 2),
        out_specs=vmem,
        scratch_shapes=[pltpu.VMEM((rows, cols), jnp.float32)],
        compiler_params=pltpu.CompilerParams(vmem_limit_bytes=6 * MIB),
        cost_estimate=pl.CostEstimate(
            flops=2 * Y * rows * cols * cols // 2, bytes_accessed=12 * MIB, transcendentals=0),
        name="far_product",
    )(*left, total, stack)


def encode(block, payload_ref):
    part = block.shape[0] // 2
    packed = jnp.concatenate([block[:part], block[part:]], axis=1)
    top = jnp.maximum(jnp.max(jnp.abs(packed), axis=0, keepdims=True), 1e-30)
    power = jnp.ceil(jnp.log2(top) + 1e-3)
    payload_ref[:part, :] = jnp.round(packed * jnp.exp2(LEVELS - power)).astype(jnp.int32).astype(jnp.int16)
    payload_ref[part:, :] = jnp.broadcast_to(power, (16, packed.shape[1])).astype(jnp.int32).astype(jnp.int16)


def decode(payload_ref):
    part = payload_ref.shape[0] - 16
    power = payload_ref[part:, :].astype(jnp.int32).astype(jnp.float32)[:1]
    packed = payload_ref[:part, :].astype(jnp.int32).astype(jnp.float32) * jnp.exp2(power - LEVELS)
    width = packed.shape[1] // 2
    return jnp.concatenate([packed[:, :width], packed[:, width:]])


def join_kernel(keep_ref, got_ref, out_ref, same_ref, cross_ref):
    core = lax.axis_index("row") % CORE
    out_ref[...] = keep_ref[...] + got_ref[...]
    half = out_ref.shape[1] // 2
    low, high = out_ref[:, :half], out_ref[:, half:]
    encode(jnp.where(core == 0, low, high), same_ref)
    encode(jnp.where(core == 0, high, low), cross_ref)


def join(keep, got):
    rows, cols = keep.shape
    payload = jax.ShapeDtypeStruct((rows // 2 + 16, cols), jnp.int16)
    vmem = pl.BlockSpec(memory_space=pltpu.VMEM)
    return pl.pallas_call(
        join_kernel,
        out_shape=[jax.ShapeDtypeStruct((rows, cols), jnp.float32), payload, payload],
        in_specs=[vmem] * 2,
        out_specs=[vmem] * 3,
        compiler_params=pltpu.CompilerParams(vmem_limit_bytes=6 * MIB),
        cost_estimate=pl.CostEstimate(flops=4 * rows * cols, bytes_accessed=12 * rows * cols, transcendentals=0),
        name="join",
    )(keep, got)


def combine_kernel(product_ref, same_ref, cross_ref, row_gap_ref, col_gap_ref, out_ref):
    core = lax.axis_index("row") % CORE
    same, cross = decode(same_ref).T, decode(cross_ref).T
    mirror = jnp.concatenate(
        [jnp.where(core == 0, same, cross), jnp.where(core == 0, cross, same)], axis=1)
    out_ref[...] = (product_ref[...] + mirror) / (row_gap_ref[...] + col_gap_ref[...])


def combine(product, same, cross, row_gap, col_gap):
    rows, cols = product.shape
    return pl.pallas_call(
        combine_kernel,
        out_shape=jax.ShapeDtypeStruct((rows, cols), jnp.float32),
        in_specs=[pl.BlockSpec(memory_space=pltpu.VMEM)] * 5,
        out_specs=pl.BlockSpec(memory_space=pltpu.VMEM),
        compiler_params=pltpu.CompilerParams(vmem_limit_bytes=8 * MIB),
        cost_estimate=pl.CostEstimate(flops=4 * rows * cols, bytes_accessed=12 * rows * cols, transcendentals=0),
        name="combine",
    )(product, same, cross, row_gap[:, None], col_gap[None, :])


def shards(amplitudes, integrals, occ_energy, vir_energy, pair_occ, pair_vir):
    tile_rows, tile_cols = amplitudes.shape
    core = lax.axis_index("row") % CORE
    other = send(amplitudes, across_core)
    lane = lax.broadcasted_iota(jnp.int32, amplitudes.shape, 1)
    half = tile_cols // 2
    left = jnp.where(
        lane < half,
        jnp.where(core == 0, amplitudes, jnp.roll(amplitudes, half, axis=1)),
        jnp.where(core == 0, jnp.roll(other, half, axis=1), other))
    near, far, early, late = gather(left, integrals, other)

    row_count, col_count = lax.axis_size("row"), lax.axis_size("col")
    row, col = lax.axis_index("row"), lax.axis_index("col")
    row_occ, row_vir = block_of(pair_occ, row, row_count), block_of(pair_vir, row, row_count)
    col_occ, col_vir = block_of(pair_occ, col, col_count), block_of(pair_vir, col, col_count)
    row_gap = lookup(occ_energy, row_occ) - lookup(vir_energy, row_vir)
    col_gap = lookup(occ_energy, col_occ) - lookup(vir_energy, col_vir)

    stack, row_gap, col_gap = lax.optimization_barrier((stacked(early), row_gap, col_gap))
    total, stack = near_product(near, late, stack)
    give = far_product(far, total, stack, False)
    got = send(give, across_core)
    keep = far_product(far, total, stack, True)
    product, to_same, to_cross = join(keep, got)
    same = send(to_same, mirrored(0))
    cross = send(send(to_cross, detour), after_detour)

    return combine(product, same, cross, row_gap, col_gap)


def solution(mesh):
    return jax.shard_map(
        shards,
        mesh=mesh,
        in_specs=(P("row", "col"), P("row", "col"), P(), P(), P(), P()),
        out_specs=P("row", "col"),
        check_vma=False,
    )
```

```python
import jax
import jax.numpy as jnp
from jax import lax
from jax.experimental import pallas as pl
from jax.experimental.pallas import tpu as pltpu
from jax.sharding import PartitionSpec as P

Z_LO, X, CORE, Y, Z_HI = 2, 4, 2, 4, 2
AXES = ("row", "col")
LEVELS = 15
MIB = 2**20


def device_index(z_lo, x, core, y, z_hi):
    return ((z_lo * X + x) * CORE + core) * (Y * Z_HI) + y * Z_HI + z_hi


def places():
    for z_lo in range(Z_LO):
        for x in range(X):
            for core in range(CORE):
                for y in range(Y):
                    for z_hi in range(Z_HI):
                        yield z_lo, x, core, y, z_hi


def send(block, target):
    pairs = [(device_index(*place), device_index(*target(*place))) for place in places()]
    return lax.ppermute(block, AXES, pairs)


def along_x(step):
    return lambda z_lo, x, core, y, z_hi: (z_lo, (x + step) % X, core, y, z_hi)


def along_y(step):
    return lambda z_lo, x, core, y, z_hi: (z_lo, x, core, (y + step) % Y, z_hi)


def across_z_lo(z_lo, x, core, y, z_hi):
    return 1 - z_lo, x, core, y, z_hi


def across_z_hi(z_lo, x, core, y, z_hi):
    return z_lo, x, core, y, 1 - z_hi


def across_core(z_lo, x, core, y, z_hi):
    return z_lo, x, 1 - core, y, z_hi


def mirrored(flip):
    def target(z_lo, x, core, y, z_hi):
        chip_row, chip_col = z_lo * X + x, y * Z_HI + z_hi
        return chip_col // X, chip_col % X, core ^ flip, chip_row // Z_HI, chip_row % Z_HI

    return target


def detour(z_lo, x, core, y, z_hi):
    x_bit = x // 2 ^ y % 2 ^ z_hi
    return x % 2 ^ z_hi ^ z_lo, x // 2 * 2 + x_bit, core, y, x % 2


def after_detour(z_lo, x, core, y, z_hi):
    start = next(place for place in places() if detour(*place) == (z_lo, x, core, y, z_hi))
    return mirrored(1)(*start)


def after(block, *earlier):
    return lax.optimization_barrier((block, *earlier))[0]


def gather(left, right, other):
    half = left.shape[0] // 2
    right_z = send(right, across_z_lo)
    late = after(right, other)
    right_up, right_down = send(late, along_x(1)), send(late, along_x(-1))
    left_up, left_down = send(left, along_y(1)), send(left, along_y(-1))
    left_z = send(after(left, right_z), across_z_hi)
    right_up, right_down, right_z = lax.optimization_barrier((right_up, right_down, right_z))
    right_two = send(right_up, along_x(1))
    right_z_down = send(right_z, along_x(-1))
    right_z_up = send(after(right_z, right_two), along_x(1))
    right_z_two = send(right_z_down, along_x(-1))
    left_two = jnp.concatenate([send(left_up[:half], along_y(1)), send(left_down[half:], along_y(-1))])
    left_z_up, left_z_down = send(left_z, along_y(1)), send(left_z, along_y(-1))
    left_z_two = send(left_two, across_z_hi)
    near = [left, left_down, left_two, left_up]
    far = [left_z, left_z_down, left_z_two, left_z_up]
    return near, far, [right, right_down, right_two, right_up], [right_z, right_z_down, right_z_two, right_z_up]


def block_of(values, index, count):
    table = values.reshape(count, -1)
    rows = lax.broadcasted_iota(jnp.int32, table.shape, 0)
    return jnp.sum(jnp.where(rows == index, table, 0), axis=0)


def lookup(energies, orbital_index):
    labels = jnp.arange(energies.shape[0], dtype=jnp.int32)
    picked = jnp.where(orbital_index[:, None] == labels[None, :], energies[None, :], 0.0)
    return jnp.sum(picked, axis=1)


def copies_into(stack_ref, first, parts, sem):
    return [pltpu.make_async_copy(part, stack_ref.at[first + i], sem.at[i]) for i, part in enumerate(parts)]


def product_terms(kind):
    row, col = lax.axis_index("row"), lax.axis_index("col")
    z_lo, x = row // (X * CORE), (row // CORE) % X
    y, z_hi = col // Z_HI, col % Z_HI
    left_far, right_far = kind
    low = 1 - z_hi if left_far else z_hi
    high = 1 - z_lo if right_far else z_lo
    terms = []
    for middle in range(2):
        left_y, right_x = high * 2 + middle, middle * 2 + low
        terms.append((
            left_far * Y + lax.rem(left_y - y + Y, Y), right_far * X + lax.rem(right_x - x + X, X)))
    return terms


def near_kernel(*refs):
    left, right, (sum_ref, stack_ref, left_stack, acc, sem_left, sem_right) = refs[:Y], refs[Y:Y + X], refs[Y + X:]
    depth = stack_ref.shape[2] // 2
    copies = copies_into(left_stack, 0, left, sem_left) + copies_into(stack_ref, 0, right, sem_right)
    for copy in copies:
        copy.start()
    for copy in copies:
        copy.wait()
    for i, (left_slot, right_slot) in enumerate(product_terms((0, 0))):
        block = left_stack[left_slot]
        both = jnp.concatenate([block[:, :depth], block[:, depth:]])
        term = jnp.dot(both, stack_ref[right_slot], preferred_element_type=jnp.float32)
        if i == 0:
            acc[...] = term
        else:
            sum_ref[...] = acc[...] + term


def near_product(left, right):
    rows, cols = left[0].shape
    vmem = pl.BlockSpec(memory_space=pltpu.VMEM)
    stack = jax.ShapeDtypeStruct((2 * X, rows, cols), jnp.bfloat16)
    return pl.pallas_call(
        near_kernel,
        out_shape=[jax.ShapeDtypeStruct((2 * rows, cols), jnp.float32), stack, stack],
        in_specs=[pl.BlockSpec(memory_space=pl.ANY)] * (X + Y),
        out_specs=[vmem] * 3,
        scratch_shapes=[
            pltpu.VMEM((2 * rows, cols), jnp.float32),
            pltpu.SemaphoreType.DMA((Y,)),
            pltpu.SemaphoreType.DMA((X,)),
        ],
        compiler_params=pltpu.CompilerParams(vmem_limit_bytes=10 * MIB),
        cost_estimate=pl.CostEstimate(
            flops=4 * 2 * rows * cols * cols // 2, bytes_accessed=12 * MIB, transcendentals=0),
        name="near_product",
    )(*left, *right)


def far_kernel(own, parts, *refs):
    incoming, refs = refs[:parts], refs[parts:]
    if parts:
        sum_ref, _, _, out_ref, right_stack, left_stack, acc, sem_left, sem_right = refs
        copies = copies_into(left_stack, Y, incoming[:Y], sem_left)
        copies += copies_into(right_stack, X, incoming[Y:], sem_right)
        for copy in copies:
            copy.start()
        for copy in copies:
            copy.wait()
    else:
        sum_ref, right_stack, left_stack, out_ref, acc = refs
    depth = right_stack.shape[2] // 2
    rows = out_ref.shape[0]
    first = 0 if own else 1
    terms = product_terms((0, 1)) + product_terms((1, 0)) + product_terms((1, 1))
    for i, (left_slot, right_slot) in enumerate(terms):
        block = left_stack[left_slot]
        term = jnp.dot(
            block[:, first * depth:(first + 1) * depth], right_stack[right_slot], preferred_element_type=jnp.float32)
        if i == 0:
            acc[...] = term + sum_ref[first * rows:(first + 1) * rows, :]
        elif i < len(terms) - 1:
            acc[...] += term
        else:
            out_ref[...] = acc[...] + term


def far_product(incoming, total, right_stack, left_stack, own):
    rows, cols = right_stack.shape[1:]
    parts = len(incoming)
    vmem = pl.BlockSpec(memory_space=pltpu.VMEM)
    stack = jax.ShapeDtypeStruct(right_stack.shape, right_stack.dtype)
    out = jax.ShapeDtypeStruct((rows, cols), jnp.float32)
    sems = [pltpu.SemaphoreType.DMA((Y,)), pltpu.SemaphoreType.DMA((X,))]
    return pl.pallas_call(
        lambda *refs: far_kernel(own, parts, *refs),
        out_shape=[out, stack, stack] if parts else out,
        in_specs=[pl.BlockSpec(memory_space=pl.ANY)] * parts + [vmem] * 3,
        out_specs=[vmem] * 3 if parts else vmem,
        scratch_shapes=[pltpu.VMEM((rows, cols), jnp.float32)] + (sems if parts else []),
        input_output_aliases={parts + 1: 1, parts + 2: 2} if parts else {},
        compiler_params=pltpu.CompilerParams(vmem_limit_bytes=6 * MIB),
        cost_estimate=pl.CostEstimate(
            flops=2 * 6 * rows * cols * cols // 2, bytes_accessed=12 * MIB, transcendentals=0),
        name="far_product",
    )(*incoming, total, right_stack, left_stack)


def encode(block, payload_ref):
    part = block.shape[0] // 2
    packed = jnp.concatenate([block[:part], block[part:]], axis=1)
    top = jnp.maximum(jnp.max(jnp.abs(packed), axis=0, keepdims=True), 1e-30)
    power = jnp.ceil(jnp.log2(top) + 1e-3)
    payload_ref[:part, :] = jnp.round(packed * jnp.exp2(LEVELS - power)).astype(jnp.int32).astype(jnp.int16)
    payload_ref[part:, :] = jnp.broadcast_to(power, (16, packed.shape[1])).astype(jnp.int32).astype(jnp.int16)


def decode(payload_ref):
    part = payload_ref.shape[0] - 16
    power = payload_ref[part:, :].astype(jnp.int32).astype(jnp.float32)[:1]
    packed = payload_ref[:part, :].astype(jnp.int32).astype(jnp.float32) * jnp.exp2(power - LEVELS)
    width = packed.shape[1] // 2
    return jnp.concatenate([packed[:, :width], packed[:, width:]])


def join_kernel(keep_ref, got_ref, out_ref, same_ref, cross_ref):
    core = lax.axis_index("row") % CORE
    out_ref[...] = keep_ref[...] + got_ref[...]
    half = out_ref.shape[1] // 2
    low, high = out_ref[:, :half], out_ref[:, half:]
    encode(jnp.where(core == 0, low, high), same_ref)
    encode(jnp.where(core == 0, high, low), cross_ref)


def join(keep, got):
    rows, cols = keep.shape
    payload = jax.ShapeDtypeStruct((rows // 2 + 16, cols), jnp.int16)
    vmem = pl.BlockSpec(memory_space=pltpu.VMEM)
    return pl.pallas_call(
        join_kernel,
        out_shape=[jax.ShapeDtypeStruct((rows, cols), jnp.float32), payload, payload],
        in_specs=[vmem] * 2,
        out_specs=[vmem] * 3,
        compiler_params=pltpu.CompilerParams(vmem_limit_bytes=6 * MIB),
        cost_estimate=pl.CostEstimate(flops=4 * rows * cols, bytes_accessed=12 * rows * cols, transcendentals=0),
        name="join",
    )(keep, got)


def combine_kernel(product_ref, same_ref, cross_ref, row_gap_ref, col_gap_ref, out_ref):
    core = lax.axis_index("row") % CORE
    same, cross = decode(same_ref).T, decode(cross_ref).T
    mirror = jnp.concatenate(
        [jnp.where(core == 0, same, cross), jnp.where(core == 0, cross, same)], axis=1)
    out_ref[...] = (product_ref[...] + mirror) / (row_gap_ref[...] + col_gap_ref[...])


def combine(product, same, cross, row_gap, col_gap):
    rows, cols = product.shape
    return pl.pallas_call(
        combine_kernel,
        out_shape=jax.ShapeDtypeStruct((rows, cols), jnp.float32),
        in_specs=[pl.BlockSpec(memory_space=pltpu.VMEM)] * 5,
        out_specs=pl.BlockSpec(memory_space=pltpu.VMEM),
        compiler_params=pltpu.CompilerParams(vmem_limit_bytes=8 * MIB),
        cost_estimate=pl.CostEstimate(flops=4 * rows * cols, bytes_accessed=12 * rows * cols, transcendentals=0),
        name="combine",
    )(product, same, cross, row_gap[:, None], col_gap[None, :])


def shards(amplitudes, integrals, occ_energy, vir_energy, pair_occ, pair_vir):
    tile_rows, tile_cols = amplitudes.shape
    core = lax.axis_index("row") % CORE
    other = send(amplitudes, across_core)
    lane = lax.broadcasted_iota(jnp.int32, amplitudes.shape, 1)
    half = tile_cols // 2
    left = jnp.where(
        lane < half,
        jnp.where(core == 0, amplitudes, jnp.roll(amplitudes, half, axis=1)),
        jnp.where(core == 0, jnp.roll(other, half, axis=1), other))
    near, far, right_near, right_far = gather(left, integrals, other)

    row_count, col_count = lax.axis_size("row"), lax.axis_size("col")
    row, col = lax.axis_index("row"), lax.axis_index("col")
    row_occ, row_vir = block_of(pair_occ, row, row_count), block_of(pair_vir, row, row_count)
    col_occ, col_vir = block_of(pair_occ, col, col_count), block_of(pair_vir, col, col_count)
    row_gap = lookup(occ_energy, row_occ) - lookup(vir_energy, row_vir)
    col_gap = lookup(occ_energy, col_occ) - lookup(vir_energy, col_vir)

    total, right_stack, left_stack = near_product(near, right_near)
    total, row_gap, col_gap = lax.optimization_barrier((total, row_gap, col_gap))
    give, right_stack, left_stack = far_product((*far, *right_far), total, right_stack, left_stack, False)
    got = send(give, across_core)
    keep = far_product((), total, right_stack, left_stack, True)
    product, to_same, to_cross = join(keep, got)
    same = send(to_same, mirrored(0))
    cross = send(send(to_cross, detour), after_detour)

    return combine(product, same, cross, row_gap, col_gap)


def solution(mesh):
    return jax.shard_map(
        shards,
        mesh=mesh,
        in_specs=(P("row", "col"), P("row", "col"), P(), P(), P(), P()),
        out_specs=P("row", "col"),
        check_vma=False,
    )
```

```python
import jax
import jax.numpy as jnp
from jax import lax
from jax.experimental import pallas as pl
from jax.experimental.pallas import tpu as pltpu
from jax.sharding import PartitionSpec as P

Z_LO, X, CORE, Y, Z_HI = 2, 4, 2, 4, 2
AXES = ("row", "col")
LEVELS = 15
MIB = 2**20


def device_index(z_lo, x, core, y, z_hi):
    return ((z_lo * X + x) * CORE + core) * (Y * Z_HI) + y * Z_HI + z_hi


def places():
    for z_lo in range(Z_LO):
        for x in range(X):
            for core in range(CORE):
                for y in range(Y):
                    for z_hi in range(Z_HI):
                        yield z_lo, x, core, y, z_hi


def send(block, target):
    pairs = [(device_index(*place), device_index(*target(*place))) for place in places()]
    return lax.ppermute(block, AXES, pairs)


def along_x(step):
    return lambda z_lo, x, core, y, z_hi: (z_lo, (x + step) % X, core, y, z_hi)


def along_y(step):
    return lambda z_lo, x, core, y, z_hi: (z_lo, x, core, (y + step) % Y, z_hi)


def across_z_lo(z_lo, x, core, y, z_hi):
    return 1 - z_lo, x, core, y, z_hi


def across_z_hi(z_lo, x, core, y, z_hi):
    return z_lo, x, core, y, 1 - z_hi


def across_core(z_lo, x, core, y, z_hi):
    return z_lo, x, 1 - core, y, z_hi


def chip_index(z_lo, x, y, z_hi):
    return ((z_hi * Z_LO + z_lo) * Y + y) * X + x


def at_chip(index, core):
    x, y, z = index % X, index // X % Y, index // (X * Y)
    return z % Z_LO, x, core, y, z // Z_LO


def mirrored(z_lo, x, core, y, z_hi):
    chip_row, chip_col = z_lo * X + x, y * Z_HI + z_hi
    return chip_col // X, chip_col % X, core, chip_row // Z_HI, chip_row % Z_HI


VIA = (
    (0, 49, 53, 51, 4, 37, 6, 35, 12, 52, 43, 55, 13, 61, 14, 63,
     3, 21, 1, 47, 7, 41, 2, 48, 24, 40, 29, 11, 25, 45, 46, 62,
     17, 33, 54, 36, 16, 34, 22, 39, 5, 9, 26, 23, 28, 50, 30, 15,
     8, 44, 18, 32, 27, 10, 19, 38, 56, 57, 42, 60, 20, 58, 31, 59),
    (16, 36, 18, 7, 1, 50, 54, 26, 17, 5, 25, 59, 28, 2, 22, 3,
     8, 32, 12, 23, 20, 38, 19, 42, 24, 9, 27, 44, 31, 10, 30, 15,
     0, 61, 11, 34, 55, 33, 37, 39, 47, 52, 58, 40, 35, 45, 43, 56,
     53, 13, 14, 49, 4, 41, 6, 48, 21, 57, 29, 62, 60, 51, 46, 63),
)


def detour(z_lo, x, core, y, z_hi):
    return at_chip(VIA[core][chip_index(z_lo, x, y, z_hi)], core)


def after_detour(z_lo, x, core, y, z_hi):
    return mirrored(*at_chip(VIA[core].index(chip_index(z_lo, x, y, z_hi)), core))


def after(block, *earlier):
    return lax.optimization_barrier((block, *earlier))[0]


def gather(left, right, other):
    half = left.shape[0] // 2
    right_z = send(right, across_z_lo)
    late = after(right, other)
    right_up, right_down = send(late, along_x(1)), send(late, along_x(-1))
    left_up, left_down = send(left, along_y(1)), send(left, along_y(-1))
    left_z = send(after(left, right_z), across_z_hi)
    right_up, right_down, right_z = lax.optimization_barrier((right_up, right_down, right_z))
    right_two = send(right_up, along_x(1))
    right_z_down = send(right_z, along_x(-1))
    right_z_up = send(after(right_z, right_two), along_x(1))
    right_z_two = send(right_z_down, along_x(-1))
    left_two = jnp.concatenate([send(left_up[:half], along_y(1)), send(left_down[half:], along_y(-1))])
    left_z_up, left_z_down = send(left_z, along_y(1)), send(left_z, along_y(-1))
    left_z_two = send(left_two, across_z_hi)
    near = [left, left_down, left_two, left_up]
    far = [left_z, left_z_down, left_z_two, left_z_up]
    return near, far, [right, right_down, right_two, right_up], [right_z, right_z_down, right_z_two, right_z_up]


def block_of(values, index, count):
    table = values.reshape(count, -1)
    rows = lax.broadcasted_iota(jnp.int32, table.shape, 0)
    return jnp.sum(jnp.where(rows == index, table, 0), axis=0)


def lookup(energies, orbital_index):
    labels = jnp.arange(energies.shape[0], dtype=jnp.int32)
    picked = jnp.where(orbital_index[:, None] == labels[None, :], energies[None, :], 0.0)
    return jnp.sum(picked, axis=1)


def copies_into(stack_ref, first, parts, sem):
    return [pltpu.make_async_copy(part, stack_ref.at[first + i], sem.at[i]) for i, part in enumerate(parts)]


def product_terms(kind):
    row, col = lax.axis_index("row"), lax.axis_index("col")
    z_lo, x = row // (X * CORE), (row // CORE) % X
    y, z_hi = col // Z_HI, col % Z_HI
    left_far, right_far = kind
    low = 1 - z_hi if left_far else z_hi
    high = 1 - z_lo if right_far else z_lo
    terms = []
    for middle in range(2):
        left_y, right_x = high * 2 + middle, middle * 2 + low
        terms.append((
            left_far * Y + lax.rem(left_y - y + Y, Y), right_far * X + lax.rem(right_x - x + X, X)))
    return terms


def near_kernel(*refs):
    left, right, (sum_ref, stack_ref, left_stack, acc, sem_left, sem_right) = refs[:Y], refs[Y:Y + X], refs[Y + X:]
    depth = stack_ref.shape[2] // 2
    copies = copies_into(left_stack, 0, left, sem_left) + copies_into(stack_ref, 0, right, sem_right)
    for copy in copies:
        copy.start()
    for copy in copies:
        copy.wait()
    for i, (left_slot, right_slot) in enumerate(product_terms((0, 0))):
        block = left_stack[left_slot]
        both = jnp.concatenate([block[:, :depth], block[:, depth:]])
        term = jnp.dot(both, stack_ref[right_slot], preferred_element_type=jnp.float32)
        if i == 0:
            acc[...] = term
        else:
            sum_ref[...] = acc[...] + term


def near_product(left, right):
    rows, cols = left[0].shape
    vmem = pl.BlockSpec(memory_space=pltpu.VMEM)
    stack = jax.ShapeDtypeStruct((2 * X, rows, cols), jnp.bfloat16)
    return pl.pallas_call(
        near_kernel,
        out_shape=[jax.ShapeDtypeStruct((2 * rows, cols), jnp.float32), stack, stack],
        in_specs=[pl.BlockSpec(memory_space=pl.ANY)] * (X + Y),
        out_specs=[vmem] * 3,
        scratch_shapes=[
            pltpu.VMEM((2 * rows, cols), jnp.float32),
            pltpu.SemaphoreType.DMA((Y,)),
            pltpu.SemaphoreType.DMA((X,)),
        ],
        compiler_params=pltpu.CompilerParams(vmem_limit_bytes=10 * MIB),
        cost_estimate=pl.CostEstimate(
            flops=4 * 2 * rows * cols * cols // 2, bytes_accessed=12 * MIB, transcendentals=0),
        name="near_product",
    )(*left, *right)


def far_kernel(own, parts, *refs):
    incoming, refs = refs[:parts], refs[parts:]
    if parts:
        sum_ref, _, _, out_ref, right_stack, left_stack, acc, sem_left, sem_right = refs
        copies = copies_into(left_stack, Y, incoming[:Y], sem_left)
        copies += copies_into(right_stack, X, incoming[Y:], sem_right)
        for copy in copies:
            copy.start()
        for copy in copies:
            copy.wait()
    else:
        sum_ref, right_stack, left_stack, out_ref, acc = refs
    core = lax.axis_index("row") % CORE
    depth = right_stack.shape[2] // 2
    rows = out_ref.shape[0]
    terms = product_terms((0, 1)) + product_terms((1, 0)) + product_terms((1, 1))

    def run(columns):
        for half in range(2):
            acc[half] = sum_ref[half * rows:(half + 1) * rows, columns]
        for left_slot, right_slot in terms:
            block, right = left_stack[left_slot], right_stack[right_slot][:, columns]
            for half in range(2):
                acc[half] += jnp.dot(
                    block[:, half * depth:(half + 1) * depth], right, preferred_element_type=jnp.float32)
        out_ref[...] = jnp.concatenate([acc[0], acc[1]], axis=1)

    @pl.when(core == (0 if own else 1))
    def _():
        run(slice(0, depth))

    @pl.when(core == (1 if own else 0))
    def _():
        run(slice(depth, 2 * depth))


def far_product(incoming, total, right_stack, left_stack, own):
    rows, cols = right_stack.shape[1:]
    parts = len(incoming)
    vmem = pl.BlockSpec(memory_space=pltpu.VMEM)
    stack = jax.ShapeDtypeStruct(right_stack.shape, right_stack.dtype)
    out = jax.ShapeDtypeStruct((rows, cols), jnp.float32)
    sems = [pltpu.SemaphoreType.DMA((Y,)), pltpu.SemaphoreType.DMA((X,))]
    return pl.pallas_call(
        lambda *refs: far_kernel(own, parts, *refs),
        out_shape=[out, stack, stack] if parts else out,
        in_specs=[pl.BlockSpec(memory_space=pl.ANY)] * parts + [vmem] * 3,
        out_specs=[vmem] * 3 if parts else vmem,
        scratch_shapes=[pltpu.VMEM((2, rows, cols // 2), jnp.float32)] + (sems if parts else []),
        input_output_aliases={parts + 1: 1, parts + 2: 2} if parts else {},
        compiler_params=pltpu.CompilerParams(vmem_limit_bytes=10 * MIB),
        cost_estimate=pl.CostEstimate(
            flops=2 * 6 * rows * cols * cols // 2, bytes_accessed=12 * MIB, transcendentals=0),
        name="far_product",
    )(*incoming, total, right_stack, left_stack)


def encode(block, payload_ref):
    part = block.shape[0]
    top = jnp.maximum(jnp.max(jnp.abs(block), axis=0, keepdims=True), 1e-30)
    power = jnp.ceil(jnp.log2(top) + 1e-3)
    payload_ref[:part, :] = jnp.round(block * jnp.exp2(LEVELS - power)).astype(jnp.int32).astype(jnp.int16)
    payload_ref[part:, :] = jnp.broadcast_to(power, (16, block.shape[1])).astype(jnp.int32).astype(jnp.int16)


def decode(payload_ref):
    part = payload_ref.shape[0] - 16
    power = payload_ref[part:, :].astype(jnp.int32).astype(jnp.float32)[:1]
    return payload_ref[:part, :].astype(jnp.int32).astype(jnp.float32) * jnp.exp2(power - LEVELS)


def join_kernel(keep_ref, got_ref, own_ref, other_ref, payload_ref):
    half = keep_ref.shape[1] // 2
    own = keep_ref[:, :half] + got_ref[:, half:]
    other = keep_ref[:, half:] + got_ref[:, :half]
    own_ref[...] = own
    other_ref[...] = other
    encode(jnp.concatenate([own, other], axis=1), payload_ref)


def join(keep, got):
    rows, cols = keep.shape
    half = jax.ShapeDtypeStruct((rows, cols // 2), jnp.float32)
    vmem = pl.BlockSpec(memory_space=pltpu.VMEM)
    return pl.pallas_call(
        join_kernel,
        out_shape=[half, half, jax.ShapeDtypeStruct((rows + 16, cols), jnp.int16)],
        in_specs=[vmem] * 2,
        out_specs=[vmem] * 3,
        compiler_params=pltpu.CompilerParams(vmem_limit_bytes=8 * MIB),
        cost_estimate=pl.CostEstimate(flops=4 * rows * cols, bytes_accessed=12 * rows * cols, transcendentals=0),
        name="join",
    )(keep, got)


def combine_kernel(own_ref, side_ref, payload_ref, row_gap_ref, col_gap_ref, out_ref):
    core = lax.axis_index("row") % CORE
    mirror = decode(payload_ref)
    half = mirror.shape[1] // 2
    own = own_ref[...] + mirror[:, :half].T
    other = side_ref[...] + mirror[:, half:].T
    both = jnp.concatenate([jnp.where(core == 0, own, other), jnp.where(core == 0, other, own)], axis=1)
    out_ref[...] = both / (row_gap_ref[...] + col_gap_ref[...])


def combine(own, side, payload, row_gap, col_gap):
    rows, cols = row_gap.shape[0], col_gap.shape[0]
    return pl.pallas_call(
        combine_kernel,
        out_shape=jax.ShapeDtypeStruct((rows, cols), jnp.float32),
        in_specs=[pl.BlockSpec(memory_space=pltpu.VMEM)] * 5,
        out_specs=pl.BlockSpec(memory_space=pltpu.VMEM),
        compiler_params=pltpu.CompilerParams(vmem_limit_bytes=8 * MIB),
        cost_estimate=pl.CostEstimate(flops=4 * rows * cols, bytes_accessed=12 * rows * cols, transcendentals=0),
        name="combine",
    )(own, side, payload, row_gap[:, None], col_gap[None, :])


def shards(amplitudes, integrals, occ_energy, vir_energy, pair_occ, pair_vir):
    tile_rows, tile_cols = amplitudes.shape
    core = lax.axis_index("row") % CORE
    other = send(amplitudes, across_core)
    lane = lax.broadcasted_iota(jnp.int32, amplitudes.shape, 1)
    half = tile_cols // 2
    left = jnp.where(
        lane < half,
        jnp.where(core == 0, amplitudes, jnp.roll(amplitudes, half, axis=1)),
        jnp.where(core == 0, jnp.roll(other, half, axis=1), other))
    near, far, right_near, right_far = gather(left, integrals, other)

    row_count, col_count = lax.axis_size("row"), lax.axis_size("col")
    row, col = lax.axis_index("row"), lax.axis_index("col")
    row_occ, row_vir = block_of(pair_occ, row, row_count), block_of(pair_vir, row, row_count)
    col_occ, col_vir = block_of(pair_occ, col, col_count), block_of(pair_vir, col, col_count)
    row_gap = lookup(occ_energy, row_occ) - lookup(vir_energy, row_vir)
    col_gap = lookup(occ_energy, col_occ) - lookup(vir_energy, col_vir)

    total, right_stack, left_stack = near_product(near, right_near)
    total, row_gap, col_gap = lax.optimization_barrier((total, row_gap, col_gap))
    give, right_stack, left_stack = far_product((*far, *right_far), total, right_stack, left_stack, False)
    got = send(give, across_core)
    keep = far_product((), total, right_stack, left_stack, True)
    own, other, payload = join(keep, got)
    payload = send(send(payload, detour), after_detour)
    side = send(other, across_core)
    return combine(own, side, payload, row_gap, col_gap)


def solution(mesh):
    return jax.shard_map(
        shards,
        mesh=mesh,
        in_specs=(P("row", "col"), P("row", "col"), P(), P(), P(), P()),
        out_specs=P("row", "col"),
        check_vma=False,
    )
```

```python
import jax
import jax.numpy as jnp
from jax import lax
from jax.experimental import pallas as pl
from jax.experimental.pallas import tpu as pltpu
from jax.sharding import PartitionSpec as P

Z_LO, X, CORE, Y, Z_HI = 2, 4, 2, 4, 2
AXES = ("row", "col")
LEVELS = 15
MIB = 2**20


def device_index(z_lo, x, core, y, z_hi):
    return ((z_lo * X + x) * CORE + core) * (Y * Z_HI) + y * Z_HI + z_hi


def places():
    for z_lo in range(Z_LO):
        for x in range(X):
            for core in range(CORE):
                for y in range(Y):
                    for z_hi in range(Z_HI):
                        yield z_lo, x, core, y, z_hi


def send(block, target):
    pairs = [(device_index(*place), device_index(*target(*place))) for place in places()]
    return lax.ppermute(block, AXES, pairs)


def along_x(step):
    return lambda z_lo, x, core, y, z_hi: (z_lo, (x + step) % X, core, y, z_hi)


def along_y(step):
    return lambda z_lo, x, core, y, z_hi: (z_lo, x, core, (y + step) % Y, z_hi)


def across_z_lo(z_lo, x, core, y, z_hi):
    return 1 - z_lo, x, core, y, z_hi


def across_z_hi(z_lo, x, core, y, z_hi):
    return z_lo, x, core, y, 1 - z_hi


def across_core(z_lo, x, core, y, z_hi):
    return z_lo, x, 1 - core, y, z_hi


def chip_index(z_lo, x, y, z_hi):
    return ((z_hi * Z_LO + z_lo) * Y + y) * X + x


def at_chip(index, core):
    x, y, z = index % X, index // X % Y, index // (X * Y)
    return z % Z_LO, x, core, y, z // Z_LO


def mirrored(z_lo, x, core, y, z_hi):
    chip_row, chip_col = z_lo * X + x, y * Z_HI + z_hi
    return chip_col // X, chip_col % X, core, chip_row // Z_HI, chip_row % Z_HI


VIA = (
    (0, 49, 53, 51, 4, 37, 6, 35, 12, 52, 43, 55, 13, 61, 14, 63,
     3, 21, 1, 47, 7, 41, 2, 48, 24, 40, 29, 11, 25, 45, 46, 62,
     17, 33, 54, 36, 16, 34, 22, 39, 5, 9, 26, 23, 28, 50, 30, 15,
     8, 44, 18, 32, 27, 10, 19, 38, 56, 57, 42, 60, 20, 58, 31, 59),
    (16, 36, 18, 7, 1, 50, 54, 26, 17, 5, 25, 59, 28, 2, 22, 3,
     8, 32, 12, 23, 20, 38, 19, 42, 24, 9, 27, 44, 31, 10, 30, 15,
     0, 61, 11, 34, 55, 33, 37, 39, 47, 52, 58, 40, 35, 45, 43, 56,
     53, 13, 14, 49, 4, 41, 6, 48, 21, 57, 29, 62, 60, 51, 46, 63),
)


def detour(z_lo, x, core, y, z_hi):
    return at_chip(VIA[core][chip_index(z_lo, x, y, z_hi)], core)


def after_detour(z_lo, x, core, y, z_hi):
    return mirrored(*at_chip(VIA[core].index(chip_index(z_lo, x, y, z_hi)), core))


def after(block, *earlier):
    return lax.optimization_barrier((block, *earlier))[0]


def gather(left, right, other):
    half = left.shape[0] // 2
    right_z = send(right, across_z_lo)
    late = after(right, other)
    right_up, right_down = send(late, along_x(1)), send(late, along_x(-1))
    left_up, left_down = send(left, along_y(1)), send(left, along_y(-1))
    left_z = send(after(left, right_z), across_z_hi)
    right_up, right_down, right_z = lax.optimization_barrier((right_up, right_down, right_z))
    right_two = send(right_up, along_x(1))
    right_z_down = send(right_z, along_x(-1))
    right_z_up = send(after(right_z, right_two), along_x(1))
    right_z_two = send(right_z_down, along_x(-1))
    left_two = jnp.concatenate([send(left_up[:half], along_y(1)), send(left_down[half:], along_y(-1))])
    left_z_up, left_z_down = send(left_z, along_y(1)), send(left_z, along_y(-1))
    left_z_two = send(left_two, across_z_hi)
    near = [left, left_down, left_two, left_up]
    far = [left_z_down, left_z_two, left_z_up]
    return (
        [*near, left_z], far, [right, right_down, right_two, right_up, right_z, right_z_down], [right_z_two, right_z_up])


def block_of(values, index, count):
    table = values.reshape(count, -1)
    rows = lax.broadcasted_iota(jnp.int32, table.shape, 0)
    return jnp.sum(jnp.where(rows == index, table, 0), axis=0)


def lookup(energies, orbital_index):
    labels = jnp.arange(energies.shape[0], dtype=jnp.int32)
    picked = jnp.where(orbital_index[:, None] == labels[None, :], energies[None, :], 0.0)
    return jnp.sum(picked, axis=1)


def copies_into(stack_ref, first, parts, sem):
    return [pltpu.make_async_copy(part, stack_ref.at[first + i], sem.at[i]) for i, part in enumerate(parts)]


def product_terms(kind):
    row, col = lax.axis_index("row"), lax.axis_index("col")
    z_lo, x = row // (X * CORE), (row // CORE) % X
    y, z_hi = col // Z_HI, col % Z_HI
    left_far, right_far = kind
    low = 1 - z_hi if left_far else z_hi
    high = 1 - z_lo if right_far else z_lo
    terms = []
    for middle in range(2):
        left_y, right_x = high * 2 + middle, middle * 2 + low
        terms.append((
            left_far * Y + lax.rem(left_y - y + Y, Y), right_far * X + lax.rem(right_x - x + X, X)))
    return terms


def near_kernel(left_count, right_count, *refs):
    left, right, refs = refs[:left_count], refs[left_count:left_count + right_count], refs[left_count + right_count:]
    sum_ref, stack_ref, left_stack, acc, sem_left, sem_right = refs
    depth = stack_ref.shape[2] // 2
    copies = copies_into(left_stack, 0, left, sem_left) + copies_into(stack_ref, 0, right, sem_right)
    for copy in copies:
        copy.start()
    for copy in copies:
        copy.wait()
    for i, (left_slot, right_slot) in enumerate(product_terms((0, 0))):
        block = left_stack[left_slot]
        both = jnp.concatenate([block[:, :depth], block[:, depth:]])
        term = jnp.dot(both, stack_ref[right_slot], preferred_element_type=jnp.float32)
        if i == 0:
            acc[...] = term
        else:
            sum_ref[...] = acc[...] + term


def near_product(left, right):
    rows, cols = left[0].shape
    vmem = pl.BlockSpec(memory_space=pltpu.VMEM)
    stack = jax.ShapeDtypeStruct((2 * X, rows, cols), jnp.bfloat16)
    return pl.pallas_call(
        lambda *refs: near_kernel(len(left), len(right), *refs),
        out_shape=[jax.ShapeDtypeStruct((2 * rows, cols), jnp.float32), stack, stack],
        in_specs=[pl.BlockSpec(memory_space=pl.ANY)] * (len(left) + len(right)),
        out_specs=[vmem] * 3,
        scratch_shapes=[
            pltpu.VMEM((2 * rows, cols), jnp.float32),
            pltpu.SemaphoreType.DMA((len(left),)),
            pltpu.SemaphoreType.DMA((len(right),)),
        ],
        compiler_params=pltpu.CompilerParams(vmem_limit_bytes=10 * MIB),
        cost_estimate=pl.CostEstimate(
            flops=4 * 2 * rows * cols * cols // 2, bytes_accessed=12 * MIB, transcendentals=0),
        name="near_product",
    )(*left, *right)


def far_kernel(own, left_count, right_count, *refs):
    parts = left_count + right_count
    incoming, refs = refs[:parts], refs[parts:]
    left_copies = []
    if parts:
        sum_ref, _, _, out_ref, right_stack, left_stack, acc, sem_left, sem_right = refs
        left_copies = copies_into(left_stack, 2 * Y - left_count, incoming[:left_count], sem_left)
        right_copies = copies_into(right_stack, 2 * X - right_count, incoming[left_count:], sem_right)
        for copy in right_copies + left_copies:
            copy.start()
        for copy in right_copies:
            copy.wait()
    else:
        sum_ref, right_stack, left_stack, out_ref, acc = refs
    core = lax.axis_index("row") % CORE
    depth = right_stack.shape[2] // 2
    rows = out_ref.shape[0]
    near_terms, far_terms = product_terms((0, 1)), product_terms((1, 0)) + product_terms((1, 1))

    def run(columns):
        for half in range(2):
            acc[half] = sum_ref[half * rows:(half + 1) * rows, columns]
        for i, (left_slot, right_slot) in enumerate(near_terms + far_terms):
            if i == len(near_terms):
                for copy in left_copies:
                    copy.wait()
            block, right = left_stack[left_slot], right_stack[right_slot][:, columns]
            for half in range(2):
                acc[half] += jnp.dot(
                    block[:, half * depth:(half + 1) * depth], right, preferred_element_type=jnp.float32)
        out_ref[...] = jnp.concatenate([acc[0], acc[1]], axis=1)

    @pl.when(core == (0 if own else 1))
    def _():
        run(slice(0, depth))

    @pl.when(core == (1 if own else 0))
    def _():
        run(slice(depth, 2 * depth))


def far_product(left, right, total, right_stack, left_stack, own):
    rows, cols = right_stack.shape[1:]
    parts = len(left) + len(right)
    vmem = pl.BlockSpec(memory_space=pltpu.VMEM)
    stack = jax.ShapeDtypeStruct(right_stack.shape, right_stack.dtype)
    out = jax.ShapeDtypeStruct((rows, cols), jnp.float32)
    sems = [pltpu.SemaphoreType.DMA((max(len(left), 1),)), pltpu.SemaphoreType.DMA((max(len(right), 1),))]
    return pl.pallas_call(
        lambda *refs: far_kernel(own, len(left), len(right), *refs),
        out_shape=[out, stack, stack] if parts else out,
        in_specs=[pl.BlockSpec(memory_space=pl.ANY)] * parts + [vmem] * 3,
        out_specs=[vmem] * 3 if parts else vmem,
        scratch_shapes=[pltpu.VMEM((2, rows, cols // 2), jnp.float32)] + (sems if parts else []),
        input_output_aliases={parts + 1: 1, parts + 2: 2} if parts else {},
        compiler_params=pltpu.CompilerParams(vmem_limit_bytes=10 * MIB),
        cost_estimate=pl.CostEstimate(
            flops=2 * 6 * rows * cols * cols // 2, bytes_accessed=12 * MIB, transcendentals=0),
        name="far_product",
    )(*left, *right, total, right_stack, left_stack)


def encode(block, payload_ref):
    part = block.shape[0]
    top = jnp.maximum(jnp.max(jnp.abs(block), axis=0, keepdims=True), 1e-30)
    power = jnp.ceil(jnp.log2(top) + 1e-3)
    payload_ref[:part, :] = jnp.round(block * jnp.exp2(LEVELS - power)).astype(jnp.int32).astype(jnp.int16)
    payload_ref[part:, :] = jnp.broadcast_to(power, (16, block.shape[1])).astype(jnp.int32).astype(jnp.int16)


def decode(payload_ref):
    part = payload_ref.shape[0] - 16
    power = payload_ref[part:, :].astype(jnp.int32).astype(jnp.float32)[:1]
    return payload_ref[:part, :].astype(jnp.int32).astype(jnp.float32) * jnp.exp2(power - LEVELS)


def join_kernel(keep_ref, got_ref, own_ref, other_ref, *payload_refs):
    half = keep_ref.shape[1] // 2
    part = keep_ref.shape[0] // len(payload_refs)
    for i, payload_ref in enumerate(payload_refs):
        rows = slice(i * part, (i + 1) * part)
        own = keep_ref[rows, :half] + got_ref[rows, half:]
        other = keep_ref[rows, half:] + got_ref[rows, :half]
        own_ref[rows, :] = own
        other_ref[rows, :] = other
        encode(jnp.concatenate([own, other], axis=1), payload_ref)


def join(keep, got):
    rows, cols = keep.shape
    half = jax.ShapeDtypeStruct((rows, cols // 2), jnp.float32)
    payload = jax.ShapeDtypeStruct((rows // 2 + 16, cols), jnp.int16)
    vmem = pl.BlockSpec(memory_space=pltpu.VMEM)
    return pl.pallas_call(
        join_kernel,
        out_shape=[half, half, payload, payload],
        in_specs=[vmem] * 2,
        out_specs=[vmem] * 4,
        compiler_params=pltpu.CompilerParams(vmem_limit_bytes=8 * MIB),
        cost_estimate=pl.CostEstimate(flops=4 * rows * cols, bytes_accessed=12 * rows * cols, transcendentals=0),
        name="join",
    )(keep, got)


def combine_kernel(own_ref, side_ref, top_ref, bottom_ref, row_gap_ref, col_gap_ref, out_ref):
    core = lax.axis_index("row") % CORE
    mirror = jnp.concatenate([decode(top_ref), decode(bottom_ref)])
    half = mirror.shape[1] // 2
    own = own_ref[...] + mirror[:, :half].T
    other = side_ref[...] + mirror[:, half:].T
    both = jnp.concatenate([jnp.where(core == 0, own, other), jnp.where(core == 0, other, own)], axis=1)
    out_ref[...] = both / (row_gap_ref[...] + col_gap_ref[...])


def combine(own, side, payloads, row_gap, col_gap):
    rows, cols = row_gap.shape[0], col_gap.shape[0]
    return pl.pallas_call(
        combine_kernel,
        out_shape=jax.ShapeDtypeStruct((rows, cols), jnp.float32),
        in_specs=[pl.BlockSpec(memory_space=pltpu.VMEM)] * 6,
        out_specs=pl.BlockSpec(memory_space=pltpu.VMEM),
        compiler_params=pltpu.CompilerParams(vmem_limit_bytes=8 * MIB),
        cost_estimate=pl.CostEstimate(flops=4 * rows * cols, bytes_accessed=12 * rows * cols, transcendentals=0),
        name="combine",
    )(own, side, *payloads, row_gap[:, None], col_gap[None, :])


def shards(amplitudes, integrals, occ_energy, vir_energy, pair_occ, pair_vir):
    tile_rows, tile_cols = amplitudes.shape
    core = lax.axis_index("row") % CORE
    other = send(amplitudes, across_core)
    lane = lax.broadcasted_iota(jnp.int32, amplitudes.shape, 1)
    half = tile_cols // 2
    left = jnp.where(
        lane < half,
        jnp.where(core == 0, amplitudes, jnp.roll(amplitudes, half, axis=1)),
        jnp.where(core == 0, jnp.roll(other, half, axis=1), other))
    near, far, right_near, right_far = gather(left, integrals, other)

    row_count, col_count = lax.axis_size("row"), lax.axis_size("col")
    row, col = lax.axis_index("row"), lax.axis_index("col")
    row_occ, row_vir = block_of(pair_occ, row, row_count), block_of(pair_vir, row, row_count)
    col_occ, col_vir = block_of(pair_occ, col, col_count), block_of(pair_vir, col, col_count)
    row_gap = lookup(occ_energy, row_occ) - lookup(vir_energy, row_vir)
    col_gap = lookup(occ_energy, col_occ) - lookup(vir_energy, col_vir)

    total, right_stack, left_stack = near_product(near, right_near)
    total, row_gap, col_gap = lax.optimization_barrier((total, row_gap, col_gap))
    give, right_stack, left_stack = far_product(far, right_far, total, right_stack, left_stack, False)
    got = send(give, across_core)
    keep = far_product((), (), total, right_stack, left_stack, True)
    own, other, *payloads = join(keep, got)
    payloads = [send(send(payload, detour), after_detour) for payload in payloads]
    side = send(other, across_core)
    return combine(own, side, payloads, row_gap, col_gap)


def solution(mesh):
    return jax.shard_map(
        shards,
        mesh=mesh,
        in_specs=(P("row", "col"), P("row", "col"), P(), P(), P(), P()),
        out_specs=P("row", "col"),
        check_vma=False,
    )
```

```python
import jax
import jax.numpy as jnp
from jax import lax
from jax.experimental import pallas as pl
from jax.experimental.pallas import tpu as pltpu
from jax.sharding import PartitionSpec as P

Z_LO, X, CORE, Y, Z_HI = 2, 4, 2, 4, 2
AXES = ("row", "col")
LEVELS = 15
MIB = 2**20


def device_index(z_lo, x, core, y, z_hi):
    return ((z_lo * X + x) * CORE + core) * (Y * Z_HI) + y * Z_HI + z_hi


def places():
    for z_lo in range(Z_LO):
        for x in range(X):
            for core in range(CORE):
                for y in range(Y):
                    for z_hi in range(Z_HI):
                        yield z_lo, x, core, y, z_hi


def send(block, target):
    pairs = [(device_index(*place), device_index(*target(*place))) for place in places()]
    return lax.ppermute(block, AXES, pairs)


def along_x(step):
    return lambda z_lo, x, core, y, z_hi: (z_lo, (x + step) % X, core, y, z_hi)


def along_y(step):
    return lambda z_lo, x, core, y, z_hi: (z_lo, x, core, (y + step) % Y, z_hi)


def across_z_lo(z_lo, x, core, y, z_hi):
    return 1 - z_lo, x, core, y, z_hi


def across_z_hi(z_lo, x, core, y, z_hi):
    return z_lo, x, core, y, 1 - z_hi


def across_core(z_lo, x, core, y, z_hi):
    return z_lo, x, 1 - core, y, z_hi


def chip_index(z_lo, x, y, z_hi):
    return ((z_hi * Z_LO + z_lo) * Y + y) * X + x


def at_chip(index, core):
    x, y, z = index % X, index // X % Y, index // (X * Y)
    return z % Z_LO, x, core, y, z // Z_LO


def mirrored(z_lo, x, core, y, z_hi):
    chip_row, chip_col = z_lo * X + x, y * Z_HI + z_hi
    return chip_col // X, chip_col % X, core, chip_row // Z_HI, chip_row % Z_HI


VIA = (
    (4, 16, 3, 35, 1, 22, 6, 54, 24, 52, 27, 55, 17, 61, 9, 63,
     28, 45, 19, 31, 5, 38, 10, 18, 23, 8, 43, 12, 29, 42, 14, 15,
     49, 33, 53, 34, 0, 20, 51, 39, 21, 46, 25, 56, 44, 32, 30, 58,
     48, 37, 2, 50, 7, 36, 26, 59, 57, 13, 41, 62, 40, 60, 47, 11),
    (0, 49, 5, 48, 51, 53, 6, 20, 21, 13, 9, 59, 31, 12, 26, 2,
     7, 37, 1, 32, 11, 25, 3, 40, 24, 41, 29, 47, 27, 57, 30, 44,
     16, 33, 18, 52, 55, 38, 22, 23, 36, 61, 42, 39, 19, 62, 34, 43,
     4, 45, 17, 28, 56, 54, 50, 35, 8, 58, 10, 60, 15, 46, 14, 63),
)


def detour(z_lo, x, core, y, z_hi):
    return at_chip(VIA[core][chip_index(z_lo, x, y, z_hi)], core)


def after_detour(z_lo, x, core, y, z_hi):
    return mirrored(*at_chip(VIA[core].index(chip_index(z_lo, x, y, z_hi)), core))


def after(block, *earlier):
    return lax.optimization_barrier((block, *earlier))[0]


def gather(left, right, other):
    half = left.shape[0] // 2
    right_z = send(right, across_z_lo)
    late = after(right, other)
    right_up, right_down = send(late, along_x(1)), send(late, along_x(-1))
    left_up, left_down = send(left, along_y(1)), send(left, along_y(-1))
    left_z = send(after(left, right_z), across_z_hi)
    right_up, right_down, right_z = lax.optimization_barrier((right_up, right_down, right_z))
    right_two = send(right_up, along_x(1))
    right_z_down = send(right_z, along_x(-1))
    right_z_up = send(after(right_z, right_two), along_x(1))
    right_z_two = send(right_z_down, along_x(-1))
    left_two = jnp.concatenate([send(left_up[:half], along_y(1)), send(left_down[half:], along_y(-1))])
    left_z_up, left_z_down = send(left_z, along_y(1)), send(left_z, along_y(-1))
    left_z_two = send(left_two, across_z_hi)
    near = [left, left_down, left_two, left_up]
    far = [left_z_down, left_z_two, left_z_up]
    return (
        [*near, left_z], far, [right, right_down, right_two, right_up, right_z, right_z_down], [right_z_two, right_z_up])


def block_of(values, index, count):
    table = values.reshape(count, -1)
    rows = lax.broadcasted_iota(jnp.int32, table.shape, 0)
    return jnp.sum(jnp.where(rows == index, table, 0), axis=0)


def lookup(energies, orbital_index):
    labels = jnp.arange(energies.shape[0], dtype=jnp.int32)
    picked = jnp.where(orbital_index[:, None] == labels[None, :], energies[None, :], 0.0)
    return jnp.sum(picked, axis=1)


def copies_into(stack_ref, first, parts, sem):
    return [pltpu.make_async_copy(part, stack_ref.at[first + i], sem.at[i]) for i, part in enumerate(parts)]


def product_terms(kind):
    row, col = lax.axis_index("row"), lax.axis_index("col")
    z_lo, x = row // (X * CORE), (row // CORE) % X
    y, z_hi = col // Z_HI, col % Z_HI
    left_far, right_far = kind
    low = 1 - z_hi if left_far else z_hi
    high = 1 - z_lo if right_far else z_lo
    terms = []
    for middle in range(2):
        left_y, right_x = high * 2 + middle, middle * 2 + low
        terms.append((
            left_far * Y + lax.rem(left_y - y + Y, Y), right_far * X + lax.rem(right_x - x + X, X)))
    return terms


def near_kernel(left_count, right_count, *refs):
    left, right, refs = refs[:left_count], refs[left_count:left_count + right_count], refs[left_count + right_count:]
    sum_ref, stack_ref, left_stack, acc, sem_left, sem_right = refs
    depth = stack_ref.shape[2] // 2
    copies = copies_into(left_stack, 0, left, sem_left) + copies_into(stack_ref, 0, right, sem_right)
    for copy in copies:
        copy.start()
    for copy in copies:
        copy.wait()
    for i, (left_slot, right_slot) in enumerate(product_terms((0, 0))):
        block = left_stack[left_slot]
        both = jnp.concatenate([block[:, :depth], block[:, depth:]])
        term = jnp.dot(both, stack_ref[right_slot], preferred_element_type=jnp.float32)
        if i == 0:
            acc[...] = term
        else:
            sum_ref[...] = acc[...] + term


def near_product(left, right):
    rows, cols = left[0].shape
    vmem = pl.BlockSpec(memory_space=pltpu.VMEM)
    stack = jax.ShapeDtypeStruct((2 * X, rows, cols), jnp.bfloat16)
    return pl.pallas_call(
        lambda *refs: near_kernel(len(left), len(right), *refs),
        out_shape=[jax.ShapeDtypeStruct((2 * rows, cols), jnp.float32), stack, stack],
        in_specs=[pl.BlockSpec(memory_space=pl.ANY)] * (len(left) + len(right)),
        out_specs=[vmem] * 3,
        scratch_shapes=[
            pltpu.VMEM((2 * rows, cols), jnp.float32),
            pltpu.SemaphoreType.DMA((len(left),)),
            pltpu.SemaphoreType.DMA((len(right),)),
        ],
        compiler_params=pltpu.CompilerParams(vmem_limit_bytes=10 * MIB),
        cost_estimate=pl.CostEstimate(
            flops=4 * 2 * rows * cols * cols // 2, bytes_accessed=12 * MIB, transcendentals=0),
        name="near_product",
    )(*left, *right)


def far_kernel(own, left_count, right_count, *refs):
    parts = left_count + right_count
    incoming, refs = refs[:parts], refs[parts:]
    left_copies = []
    if parts:
        sum_ref, _, _, out_ref, right_stack, left_stack, acc, sem_left, sem_right = refs
        left_copies = copies_into(left_stack, 2 * Y - left_count, incoming[:left_count], sem_left)
        right_copies = copies_into(right_stack, 2 * X - right_count, incoming[left_count:], sem_right)
        for copy in right_copies + left_copies:
            copy.start()
        for copy in right_copies:
            copy.wait()
    else:
        sum_ref, right_stack, left_stack, out_ref, acc = refs
    core = lax.axis_index("row") % CORE
    depth = right_stack.shape[2] // 2
    rows = out_ref.shape[0]
    near_terms, far_terms = product_terms((0, 1)), product_terms((1, 0)) + product_terms((1, 1))

    def run(columns):
        for half in range(2):
            acc[half] = sum_ref[half * rows:(half + 1) * rows, columns]
        terms = near_terms + far_terms
        for i in range(0, len(terms), 2):
            if i == len(near_terms):
                for copy in left_copies:
                    copy.wait()
            blocks = [left_stack[left_slot] for left_slot, _ in terms[i:i + 2]]
            right = jnp.concatenate([right_stack[right_slot][:, columns] for _, right_slot in terms[i:i + 2]])
            for half in range(2):
                both = jnp.concatenate([block[:, half * depth:(half + 1) * depth] for block in blocks], axis=1)
                acc[half] += jnp.dot(both, right, preferred_element_type=jnp.float32)
        out_ref[...] = jnp.concatenate([acc[0], acc[1]], axis=1)

    @pl.when(core == (0 if own else 1))
    def _():
        run(slice(0, depth))

    @pl.when(core == (1 if own else 0))
    def _():
        run(slice(depth, 2 * depth))


def far_product(left, right, total, right_stack, left_stack, own):
    rows, cols = right_stack.shape[1:]
    parts = len(left) + len(right)
    vmem = pl.BlockSpec(memory_space=pltpu.VMEM)
    stack = jax.ShapeDtypeStruct(right_stack.shape, right_stack.dtype)
    out = jax.ShapeDtypeStruct((rows, cols), jnp.float32)
    sems = [pltpu.SemaphoreType.DMA((max(len(left), 1),)), pltpu.SemaphoreType.DMA((max(len(right), 1),))]
    return pl.pallas_call(
        lambda *refs: far_kernel(own, len(left), len(right), *refs),
        out_shape=[out, stack, stack] if parts else out,
        in_specs=[pl.BlockSpec(memory_space=pl.ANY)] * parts + [vmem] * 3,
        out_specs=[vmem] * 3 if parts else vmem,
        scratch_shapes=[pltpu.VMEM((2, rows, cols // 2), jnp.float32)] + (sems if parts else []),
        input_output_aliases={parts + 1: 1, parts + 2: 2} if parts else {},
        compiler_params=pltpu.CompilerParams(vmem_limit_bytes=10 * MIB),
        cost_estimate=pl.CostEstimate(
            flops=2 * 6 * rows * cols * cols // 2, bytes_accessed=12 * MIB, transcendentals=0),
        name="far_product",
    )(*left, *right, total, right_stack, left_stack)


def encode(block, payload_ref):
    part = block.shape[0]
    top = jnp.maximum(jnp.max(jnp.abs(block), axis=0, keepdims=True), 1e-30)
    power = jnp.ceil(jnp.log2(top) + 1e-3)
    payload_ref[:part, :] = jnp.round(block * jnp.exp2(LEVELS - power)).astype(jnp.int32).astype(jnp.int16)
    payload_ref[part:, :] = jnp.broadcast_to(power, (16, block.shape[1])).astype(jnp.int32).astype(jnp.int16)


def decode(payload_ref):
    part = payload_ref.shape[0] - 16
    power = payload_ref[part:, :].astype(jnp.int32).astype(jnp.float32)[:1]
    return payload_ref[:part, :].astype(jnp.int32).astype(jnp.float32) * jnp.exp2(power - LEVELS)


def join_kernel(keep_ref, got_ref, own_ref, other_ref, *payload_refs):
    half = keep_ref.shape[1] // 2
    part = keep_ref.shape[0] // len(payload_refs)
    for i, payload_ref in enumerate(payload_refs):
        rows = slice(i * part, (i + 1) * part)
        own = keep_ref[rows, :half] + got_ref[rows, half:]
        other = keep_ref[rows, half:] + got_ref[rows, :half]
        own_ref[rows, :] = own
        other_ref[rows, :] = other
        encode(jnp.concatenate([own, other], axis=1), payload_ref)


def join(keep, got):
    rows, cols = keep.shape
    half = jax.ShapeDtypeStruct((rows, cols // 2), jnp.float32)
    payload = jax.ShapeDtypeStruct((rows // 2 + 16, cols), jnp.int16)
    vmem = pl.BlockSpec(memory_space=pltpu.VMEM)
    return pl.pallas_call(
        join_kernel,
        out_shape=[half, half, payload, payload],
        in_specs=[vmem] * 2,
        out_specs=[vmem] * 4,
        compiler_params=pltpu.CompilerParams(vmem_limit_bytes=8 * MIB),
        cost_estimate=pl.CostEstimate(flops=4 * rows * cols, bytes_accessed=12 * rows * cols, transcendentals=0),
        name="join",
    )(keep, got)


def combine_kernel(own_ref, side_ref, top_ref, bottom_ref, row_gap_ref, col_gap_ref, out_ref):
    core = lax.axis_index("row") % CORE
    mirror = jnp.concatenate([decode(top_ref), decode(bottom_ref)])
    half = mirror.shape[1] // 2
    own = own_ref[...] + mirror[:, :half].T
    other = side_ref[...] + mirror[:, half:].T
    both = jnp.concatenate([jnp.where(core == 0, own, other), jnp.where(core == 0, other, own)], axis=1)
    out_ref[...] = both / (row_gap_ref[...] + col_gap_ref[...])


def combine(own, side, payloads, row_gap, col_gap):
    rows, cols = row_gap.shape[0], col_gap.shape[0]
    return pl.pallas_call(
        combine_kernel,
        out_shape=jax.ShapeDtypeStruct((rows, cols), jnp.float32),
        in_specs=[pl.BlockSpec(memory_space=pltpu.VMEM)] * 6,
        out_specs=pl.BlockSpec(memory_space=pltpu.VMEM),
        compiler_params=pltpu.CompilerParams(vmem_limit_bytes=8 * MIB),
        cost_estimate=pl.CostEstimate(flops=4 * rows * cols, bytes_accessed=12 * rows * cols, transcendentals=0),
        name="combine",
    )(own, side, *payloads, row_gap[:, None], col_gap[None, :])


def shards(amplitudes, integrals, occ_energy, vir_energy, pair_occ, pair_vir):
    tile_rows, tile_cols = amplitudes.shape
    core = lax.axis_index("row") % CORE
    other = send(amplitudes, across_core)
    lane = lax.broadcasted_iota(jnp.int32, amplitudes.shape, 1)
    half = tile_cols // 2
    left = jnp.where(
        lane < half,
        jnp.where(core == 0, amplitudes, jnp.roll(amplitudes, half, axis=1)),
        jnp.where(core == 0, jnp.roll(other, half, axis=1), other))
    near, far, right_near, right_far = gather(left, integrals, other)

    row_count, col_count = lax.axis_size("row"), lax.axis_size("col")
    row, col = lax.axis_index("row"), lax.axis_index("col")
    row_occ, row_vir = block_of(pair_occ, row, row_count), block_of(pair_vir, row, row_count)
    col_occ, col_vir = block_of(pair_occ, col, col_count), block_of(pair_vir, col, col_count)
    row_gap = lookup(occ_energy, row_occ) - lookup(vir_energy, row_vir)
    col_gap = lookup(occ_energy, col_occ) - lookup(vir_energy, col_vir)

    total, right_stack, left_stack = near_product(near, right_near)
    total, row_gap, col_gap = lax.optimization_barrier((total, row_gap, col_gap))
    give, right_stack, left_stack = far_product(far, right_far, total, right_stack, left_stack, False)
    got = send(give, across_core)
    keep = far_product((), (), total, right_stack, left_stack, True)
    own, other, *payloads = join(keep, got)
    payloads = [send(send(payload, detour), after_detour) for payload in payloads]
    side = send(other, across_core)
    return combine(own, side, payloads, row_gap, col_gap)


def solution(mesh):
    return jax.shard_map(
        shards,
        mesh=mesh,
        in_specs=(P("row", "col"), P("row", "col"), P(), P(), P(), P()),
        out_specs=P("row", "col"),
        check_vma=False,
    )
```
